256 devices in a mesh: trow: 16 (over x, y_lo, core), tcol: 16 (over y_hi, z).
Axes of the slice: x: 4, y: 4 (y_hi: 2, y_lo: 2; y = y_hi * 2 + y_lo), z: 8, core: 2. Of those that a mesh axis runs over, the one named last changes fastest.
Arguments:
- green_lesser: bfloat16 [2, 128, 128, 512], P(None, 'trow', 'tcol'), may hold values from -6 to 6
- green_greater: bfloat16 [2, 128, 128, 512], P(None, 'trow', 'tcol'), may hold values from -6 to 6
- lattice_map: int32 [512], replicated, may hold values from 0 to 511, each once
- time_offset: int32 [1], replicated, may hold values from 0 to 63
Outputs:
- collision_lesser: bfloat16 [2, 128, 128, 512], P(None, 'trow', 'tcol')
- collision_greater: bfloat16 [2, 128, 128, 512], P(None, 'trow', 'tcol')
The draws below stay inside these ranges and needn't reach their ends.
Inputs may be any that keep to these rules, and one draw needn't show every extreme that they name: `lattice_map`: every lattice momentum index 0 to 511 appears exactly once.
All inputs are finite; a program needn't handle non-finite values.
Results may differ from the reference program's by a relative error of at most 0.011.
Values may be sent and summed in bfloat16 or wider, within the bound.
A program may use at most 64 MiB of HBM per device.

```python
import math
import jax
import jax.numpy as jnp
from jax import lax

K = 512
PERIOD = 64
NT = 128


def block_levels(own_key, dims, shards, least, top_value):
    def one(axis_at, blocks):
        heights = jax.random.uniform(jax.random.fold_in(jax.random.fold_in(own_key, 6), axis_at), (blocks,), jnp.float32, least / len(shards), top_value / len(shards))
        return jnp.repeat(jnp.exp(heights), dims[axis_at] // blocks).reshape((-1,) + (1,) * (len(dims) - axis_at - 1))

    loudness = one(*shards[0])
    for cut in shards[1:]:
        loudness = loudness * one(*cut)
    return loudness


def bell_draw(own_key, extent, scale, reach, pieces=(), kind=jnp.bfloat16):
    array = jax.random.normal(own_key, extent, jnp.float32) * scale
    if len(pieces) > 0:
        array = block_levels(own_key, extent, pieces, -0.22, 0.18) * array
    return jnp.clip(array, min=-reach, max=reach).astype(kind)


def setup_inputs(seed: int = 0) -> dict:
    key_list = jax.random.split(jax.random.key(seed), 5)
    return {
        "green_lesser": bell_draw(key_list[0], (2, NT, NT, K), 1.0, 6.0, ((1, 16), (2, 16))),
        "green_greater": bell_draw(key_list[1], (2, NT, NT, K), 1.0, 6.0, ((1, 16), (2, 16))),
        "lattice_map": jax.random.permutation(key_list[2], K).astype(jnp.int32),
        "time_offset": jax.random.randint(key_list[3], (1,), 0, PERIOD).astype(jnp.int32),
    }


step_size = 0.01
drive_depth = 0.5

def widened(values):
    return lax.optimization_barrier(values).astype(jnp.float32)

def transform(real_part, imaginary_part, cosines, sines, sign, norm_factor):
    old_shape = real_part.shape
    flat_real = real_part.reshape(-1, old_shape[-1])
    flat_imaginary = imaginary_part.reshape(-1, old_shape[-1])
    cosine_real = jnp.dot(flat_real, cosines, preferred_element_type=jnp.float32)
    cosine_imaginary = jnp.dot(flat_imaginary, cosines, preferred_element_type=jnp.float32)
    sine_real = jnp.dot(flat_real, sines, preferred_element_type=jnp.float32)
    sine_imaginary = jnp.dot(flat_imaginary, sines, preferred_element_type=jnp.float32)
    out_real = ((cosine_real - sign * sine_imaginary) * norm_factor).reshape(old_shape).astype(jnp.bfloat16)
    out_imaginary = ((sign * sine_real + cosine_imaginary) * norm_factor).reshape(old_shape).astype(jnp.bfloat16)
    return (out_real, out_imaginary)

def second_born(first_real, first_imaginary, other_real, other_imaginary, coupling):
    square_real = first_real * first_real - first_imaginary * first_imaginary
    square_imaginary = 2.0 * first_real * first_imaginary
    out_real = coupling * (square_real * other_real - square_imaginary * other_imaginary)
    out_imaginary = coupling * (square_real * other_imaginary + square_imaginary * other_real)
    return (out_real.astype(jnp.bfloat16), out_imaginary.astype(jnp.bfloat16))

def contract(left, right):
    return jnp.einsum('kts,ksu->ktu', left, right, precision=lax.Precision.HIGHEST)

def volterra(retarded, sigma, greens, advanced):
    real_sum = contract(retarded[0], greens[0]) - contract(retarded[1], greens[1]) + contract(sigma[0], advanced[0]) - contract(sigma[1], advanced[1])
    imaginary_sum = contract(retarded[0], greens[1]) + contract(retarded[1], greens[0]) + contract(sigma[0], advanced[1]) + contract(sigma[1], advanced[0])
    return (real_sum, imaginary_sum)

def finish(parts):
    return jnp.stack([jnp.transpose(step_size * component, (1, 2, 0)) for component in parts]).astype(jnp.bfloat16)

def momentum_first(values):
    return jnp.transpose(widened(values), (2, 0, 1))

def reference(green_lesser, green_greater, lattice_map, time_offset):
    site_index = jnp.arange(K, dtype=jnp.int32)
    phases = (lattice_map[:, None] * site_index[None, :] % K).astype(jnp.float32) * (2.0 * math.pi / K)
    cosines = jnp.cos(phases).astype(jnp.bfloat16)
    sines = jnp.sin(phases).astype(jnp.bfloat16)
    norm_factor = 1.0 / math.sqrt(K)
    site_lesser = transform(green_lesser[0], green_lesser[1], cosines, sines, 1.0, norm_factor)
    site_greater = transform(green_greater[0], green_greater[1], cosines, sines, 1.0, norm_factor)
    partner = (K - site_index) % K

    def mirror_of(field):
        return jnp.swapaxes(widened(field)[:, :, partner], 0, 1)
    time_steps = jnp.arange(NT, dtype=jnp.int32)
    coupling_line = 1.0 + drive_depth * jnp.cos(((time_offset[0] + time_steps) % PERIOD).astype(jnp.float32) * (2.0 * math.pi / PERIOD))
    coupling = (coupling_line[:, None] * coupling_line[None, :])[:, :, None]
    self_lesser = second_born(widened(site_lesser[0]), widened(site_lesser[1]), mirror_of(site_greater[0]), mirror_of(site_greater[1]), coupling)
    self_greater = second_born(widened(site_greater[0]), widened(site_greater[1]), mirror_of(site_lesser[0]), mirror_of(site_lesser[1]), coupling)
    sigma_lesser = [momentum_first(component) for component in transform(self_lesser[0], self_lesser[1], cosines.T, sines.T, -1.0, norm_factor)]
    sigma_greater = [momentum_first(component) for component in transform(self_greater[0], self_greater[1], cosines.T, sines.T, -1.0, norm_factor)]
    green_less = [momentum_first(green_lesser[0]), momentum_first(green_lesser[1])]
    green_more = [momentum_first(green_greater[0]), momentum_first(green_greater[1])]
    lower_mask = time_steps[None, :] <= time_steps[:, None]
    upper_mask = time_steps[:, None] <= time_steps[None, :]
    retarded = [widened(jnp.where(lower_mask, sigma_greater[index] - sigma_lesser[index], 0.0).astype(jnp.bfloat16)) for index in range(2)]
    advanced = [widened(jnp.where(upper_mask, green_less[index] - green_more[index], 0.0).astype(jnp.bfloat16)) for index in range(2)]
    lesser_out = volterra(retarded, sigma_lesser, green_less, advanced)
    greater_out = volterra(retarded, sigma_greater, green_more, advanced)
    return (finish(lesser_out), finish(greater_out))
```

```python
import math

import jax
import jax.numpy as jnp
import numpy as np
from jax import lax
from jax.experimental import pallas as pl
from jax.experimental.pallas import tpu as pltpu
from jax.sharding import PartitionSpec as P

PERIOD = 64
STEP_SIZE = 0.01
DRIVE_DEPTH = 0.5
MESH = pl.DeviceIdType.MESH
F32 = jnp.float32
BF16 = jnp.bfloat16

N = 16
TILE = 8
K = 512
LANES = N * TILE
CELLS = TILE * TILE
NORM = 1.0 / math.sqrt(K)

NT = (((1,), (1,)), ((), ()))
NN = (((1,), (0,)), ((), ()))


def mm(left, right, dims=NN):
    return lax.dot_general(left, right, dims, preferred_element_type=F32)


def block_swap(parts):
    parts = list(parts)
    lane = lax.broadcasted_iota(jnp.int32, parts[0].shape, 1)
    bit = 1
    while bit < N:
        shift = bit * TILE
        low = (lane // shift) % 2 == 0
        for i in range(N):
            if i & bit:
                continue
            first, second = parts[i], parts[i | bit]
            parts[i] = jnp.where(low, first, pltpu.roll(second, shift, 1))
            parts[i | bit] = jnp.where(low, pltpu.roll(first, LANES - shift, 1), second)
        bit *= 2
    return parts


def kernel(
    map_ref, coupling_ref, lesser_hbm, greater_hbm, table_hbm, out_lesser, out_greater,
    green, table, perm, site, mirror_out, mirror_in, terms, spread,
    ga_out, ga_in, gb_out, gb_in, sa_out, sa_in, sb_out, sb_in, cb_out, cb_in, ca_out, ca_in,
    load_sems, pair_sems, send_sems, recv_sems,
):
    row = lax.axis_index("trow")
    col = lax.axis_index("tcol")
    apart = row != col
    barrier = pltpu.get_barrier_semaphore()

    def greet(step, carry):
        pl.semaphore_signal(
            barrier, inc=1, device_id=(lax.rem(row + step, N), col), device_id_type=MESH
        )
        pl.semaphore_signal(
            barrier, inc=1, device_id=(row, lax.rem(col + step, N)), device_id_type=MESH
        )
        return carry

    @pl.when(apart)
    def _():
        pl.semaphore_signal(barrier, inc=1, device_id=(col, row), device_id_type=MESH)

    lax.fori_loop(1, N, greet, 0)

    load_lesser = pltpu.make_async_copy(lesser_hbm, green.at[0], load_sems.at[0])
    load_greater = pltpu.make_async_copy(greater_hbm, green.at[1], load_sems.at[1])
    load_table = pltpu.make_async_copy(table_hbm, table, load_sems.at[2])
    load_lesser.start()
    load_greater.start()
    load_table.start()

    def along_rows(source, target, phase):
        def one(step, carry):
            other = lax.rem(row + step, N)
            pltpu.make_async_remote_copy(
                src_ref=source.at[other], dst_ref=target.at[row],
                send_sem=send_sems.at[phase, other], recv_sem=recv_sems.at[phase, row],
                device_id=(other, col), device_id_type=MESH,
            ).start()
            return carry

        lax.fori_loop(1, N, one, 0)
        target[pl.ds(row, 1)] = source[pl.ds(row, 1)]

    def rows_arrived(source, target, phase):
        def one(step, carry):
            other = lax.rem(row + N - step, N)
            pltpu.make_async_remote_copy(
                src_ref=source.at[other], dst_ref=target.at[other],
                send_sem=send_sems.at[phase, other], recv_sem=recv_sems.at[phase, other],
                device_id=(other, col), device_id_type=MESH,
            ).wait_recv()
            return carry

        lax.fori_loop(1, N, one, 0)

    def rows_left(source, target, phase):
        def one(step, carry):
            other = lax.rem(row + step, N)
            pltpu.make_async_remote_copy(
                src_ref=source.at[other], dst_ref=target.at[row],
                send_sem=send_sems.at[phase, other], recv_sem=recv_sems.at[phase, row],
                device_id=(other, col), device_id_type=MESH,
            ).wait_send()
            return carry

        lax.fori_loop(1, N, one, 0)

    def col_copy(source, target, phase, other, mine, scatter):
        src = source.at[other] if scatter else source.at[:, :, other]
        dst = target.at[:, :, mine] if scatter else target.at[mine]
        return pltpu.make_async_remote_copy(
            src_ref=src, dst_ref=dst,
            send_sem=send_sems.at[phase, other], recv_sem=recv_sems.at[phase, mine],
            device_id=(row, other), device_id_type=MESH,
        )

    def along_cols(source, target, phase, scatter):
        def one(step, carry):
            col_copy(source, target, phase, lax.rem(col + step, N), col, scatter).start()
            return carry

        lax.fori_loop(1, N, one, 0)
        if scatter:
            target[:, :, pl.ds(col, 1)] = source[pl.ds(col, 1)].reshape(2, 4, 1, TILE, LANES)
        else:
            target[pl.ds(col, 1)] = source[:, :, pl.ds(col, 1)].reshape(1, 2, 4, TILE, LANES)

    def cols_arrived(source, target, phase, scatter):
        def one(step, carry):
            other = lax.rem(col + N - step, N)
            src = source.at[other] if scatter else source.at[:, :, other]
            dst = target.at[:, :, other] if scatter else target.at[other]
            pltpu.make_async_remote_copy(
                src_ref=src, dst_ref=dst,
                send_sem=send_sems.at[phase, other], recv_sem=recv_sems.at[phase, other],
                device_id=(row, other), device_id_type=MESH,
            ).wait_recv()
            return carry

        lax.fori_loop(1, N, one, 0)

    def cols_left(source, target, phase, scatter):
        def one(step, carry):
            col_copy(source, target, phase, lax.rem(col + step, N), col, scatter).wait_send()
            return carry

        lax.fori_loop(1, N, one, 0)

    def rows_to_cols(arrived, outgoing):
        for half in range(2):
            for part in range(2):
                base = part * 16
                swapped = block_swap(
                    [arrived[a, half, base : base + 16, :].astype(F32) for a in range(N)]
                )
                for q in range(N):
                    start = (half * N + q) * 32 + base
                    spread[start : start + 16, :] = swapped[q]
        for m in range(32):
            picked = spread[pl.ds(m, 32, stride=32), :]
            outgoing[m // 2, m % 2] = picked.reshape(4, TILE, LANES).astype(BF16)

    def cols_to_rows(arrived, outgoing):
        for m in range(32):
            spread[m * 32 : (m + 1) * 32, :] = (
                arrived[m // 2, m % 2].astype(F32).reshape(32, LANES)
            )
        for half in range(2):
            for part in range(2):
                base = part * 16
                swapped = block_swap(
                    [
                        spread[pl.ds(base * 32 + half * N + q, 16, stride=32), :]
                        for q in range(N)
                    ]
                )
                for a in range(N):
                    outgoing[a, half, base : base + 16, :] = swapped[a].astype(BF16)

    lattice = lax.broadcasted_iota(jnp.int32, (K, K), 0)
    perm[...] = jnp.where(lattice == map_ref[...], 1.0, 0.0).astype(BF16)
    r = lax.broadcasted_iota(jnp.int32, (2 * CELLS, 2 * CELLS), 0)
    c = lax.broadcasted_iota(jnp.int32, (2 * CELLS, 2 * CELLS), 1)
    swap = jnp.where(
        (r // CELLS == c // CELLS)
        & ((r // TILE) % TILE == c % TILE)
        & (r % TILE == (c // TILE) % TILE),
        1.0,
        0.0,
    ).astype(BF16)

    load_lesser.wait()
    load_greater.wait()
    load_table.wait()
    for half in range(2):
        natural = green[half].astype(F32).reshape(2 * CELLS, K).astype(BF16)
        turned = mm(swap, natural).astype(BF16)
        by_lattice = mm(turned, perm[...], NT).astype(BF16)
        products = mm(by_lattice, table[...])
        cos_re, sin_re = products[:CELLS, :K], products[:CELLS, K:]
        cos_im, sin_im = products[CELLS:, :K], products[CELLS:, K:]
        site[half, 0] = ((cos_re - sin_im) * NORM).astype(BF16)
        site[half, 1] = ((sin_re + cos_im) * NORM).astype(BF16)
        mirror = jnp.concatenate(
            [((cos_re + sin_im) * NORM), ((cos_im - sin_re) * NORM)], axis=0
        ).astype(BF16)
        mirror_out[half] = mm(swap, mirror).astype(BF16)
        spectral = mm(perm[...], turned, NT)
        ga_out[:, half] = spectral.reshape(N, 32, LANES).astype(BF16)

    pl.semaphore_wait(barrier, 2 * (N - 1) + jnp.where(apart, 1, 0))

    @pl.when(apart)
    def _():
        pltpu.make_async_remote_copy(
            src_ref=mirror_out, dst_ref=mirror_in,
            send_sem=pair_sems.at[0], recv_sem=pair_sems.at[1],
            device_id=(col, row), device_id_type=MESH,
        ).start()

    @pl.when(jnp.logical_not(apart))
    def _():
        mirror_in[...] = mirror_out[...]

    along_rows(ga_out, ga_in, 0)

    @pl.when(apart)
    def _():
        pltpu.make_async_remote_copy(
            src_ref=mirror_out, dst_ref=mirror_in,
            send_sem=pair_sems.at[0], recv_sem=pair_sems.at[1],
            device_id=(col, row), device_id_type=MESH,
        ).wait()

    coupling = jnp.concatenate([coupling_ref[...]] * (K // LANES), axis=1)
    for half in range(2):
        first_re, first_im = site[half, 0].astype(F32), site[half, 1].astype(F32)
        other_re = mirror_in[1 - half, :CELLS, :].astype(F32)
        other_im = mirror_in[1 - half, CELLS:, :].astype(F32)
        square_re = first_re * first_re - first_im * first_im
        square_im = 2.0 * first_re * first_im
        self_re = (coupling * (square_re * other_re - square_im * other_im)).astype(BF16)
        self_im = (coupling * (square_re * other_im + square_im * other_re)).astype(BF16)
        terms[:CELLS, :K] = self_re
        terms[:CELLS, K:] = self_im
        terms[CELLS:, :K] = self_im
        terms[CELLS:, K:] = -self_re
        spectral = mm(table[...], terms[...], NT) * NORM
        sa_out[:, half] = spectral.reshape(N, 32, LANES).astype(BF16)
    along_rows(sa_out, sa_in, 1)

    rows_arrived(ga_out, ga_in, 0)
    rows_to_cols(ga_in, gb_out)
    along_cols(gb_out, gb_in, 2, True)
    rows_arrived(sa_out, sa_in, 1)
    rows_to_cols(sa_in, sb_out)
    along_cols(sb_out, sb_in, 3, True)
    cols_arrived(gb_out, gb_in, 2, True)
    cols_arrived(sb_out, sb_in, 3, True)

    down = lax.broadcasted_iota(jnp.int32, (LANES, LANES), 0)
    across = lax.broadcasted_iota(jnp.int32, (LANES, LANES), 1)
    for k in range(2):
        g = [gb_in[k, i].astype(F32).reshape(LANES, LANES) for i in range(4)]
        s = [sb_in[k, i].astype(F32).reshape(LANES, LANES) for i in range(4)]
        retarded = [jnp.where(down <= across, s[2 + i] - s[i], 0.0).astype(BF16) for i in range(2)]
        advanced = [jnp.where(across <= down, g[i] - g[2 + i], 0.0) for i in range(2)]
        for half in range(2):
            g_re, g_im = g[2 * half], g[2 * half + 1]
            left = jnp.concatenate(
                [
                    jnp.concatenate([g_re, -g_im, advanced[0], -advanced[1]], axis=1),
                    jnp.concatenate([g_im, g_re, advanced[1], advanced[0]], axis=1),
                ],
                axis=0,
            ).astype(BF16)
            right = jnp.concatenate(
                retarded + [s[2 * half].astype(BF16), s[2 * half + 1].astype(BF16)], axis=0
            )
            total = (mm(left, right) * STEP_SIZE).reshape(2, N, TILE, LANES).astype(BF16)
            cb_out[k, 2 * half] = total[0]
            cb_out[k, 2 * half + 1] = total[1]
    along_cols(cb_out, cb_in, 4, False)
    cols_arrived(cb_out, cb_in, 4, False)
    cols_to_rows(cb_in, ca_out)
    along_rows(ca_out, ca_in, 5)
    rows_arrived(ca_out, ca_in, 5)
    for half, out in enumerate((out_lesser, out_greater)):
        full = ca_in[:, half].reshape(K, LANES)
        cells = mm(swap, full, NT).astype(BF16)
        out[...] = mm(cells, perm[...]).reshape(2, TILE, TILE, K).astype(BF16)

    rows_left(ga_out, ga_in, 0)
    rows_left(sa_out, sa_in, 1)
    cols_left(gb_out, gb_in, 2, True)
    cols_left(sb_out, sb_in, 3, True)
    cols_left(cb_out, cb_in, 4, False)
    rows_left(ca_out, ca_in, 5)


def tables():
    index = np.arange(K, dtype=np.int64)
    phases = (index[:, None] * index[None, :] % K).astype(np.float32) * np.float32(
        2.0 * math.pi / K
    )
    return np.concatenate([np.cos(phases), np.sin(phases)], axis=1).astype(jnp.bfloat16)


def body(green_lesser, green_greater, lattice_map, time_offset):
    steps = jnp.arange(TILE, dtype=jnp.int32)

    def line(block):
        at = (time_offset[0] + block * TILE + steps) % PERIOD
        return 1.0 + DRIVE_DEPTH * jnp.cos(at.astype(F32) * (2.0 * math.pi / PERIOD))

    pairs = line(lax.axis_index("tcol"))[:, None] * line(lax.axis_index("trow"))[None, :]
    coupling = jnp.broadcast_to(pairs[:, :, None], (TILE, TILE, LANES)).reshape(CELLS, LANES)
    any_spec = pl.BlockSpec(memory_space=pl.ANY)
    vmem_spec = pl.BlockSpec(memory_space=pltpu.VMEM)
    tile = jax.ShapeDtypeStruct((2, TILE, TILE, K), BF16)
    by_row = pltpu.VMEM((N, 2, 32, LANES), BF16)
    by_col = pltpu.VMEM((N, 2, 4, TILE, LANES), BF16)
    window = pltpu.VMEM((2, 4, N, TILE, LANES), BF16)
    return pl.pallas_call(
        kernel,
        out_shape=(tile, tile),
        in_specs=[vmem_spec, vmem_spec, any_spec, any_spec, any_spec],
        out_specs=(vmem_spec, vmem_spec),
        scratch_shapes=[
            pltpu.VMEM((2, 2, TILE, TILE, K), BF16),
            pltpu.VMEM((K, 2 * K), BF16),
            pltpu.VMEM((K, K), BF16),
            pltpu.VMEM((2, 2, CELLS, K), BF16),
            pltpu.VMEM((2, 2 * CELLS, K), BF16),
            pltpu.VMEM((2, 2 * CELLS, K), BF16),
            pltpu.VMEM((2 * CELLS, 2 * K), BF16),
            pltpu.VMEM((1024, LANES), F32),
            by_row, by_row, by_col, window,
            by_row, by_row, by_col, window,
            window, by_col, by_row, by_row,
            pltpu.SemaphoreType.DMA((3,)),
            pltpu.SemaphoreType.DMA((2,)),
            pltpu.SemaphoreType.DMA((6, N)),
            pltpu.SemaphoreType.DMA((6, N)),
        ],
        compiler_params=pltpu.CompilerParams(
            collective_id=0, has_side_effects=True, vmem_limit_bytes=48 * 1024 * 1024
        ),
    )(lattice_map.reshape(1, K), coupling, green_lesser, green_greater, jnp.asarray(tables()))


def solution(mesh):
    in_specs = (P(None, "trow", "tcol", None), P(None, "trow", "tcol", None), P(), P())
    out_specs = (P(None, "trow", "tcol", None), P(None, "trow", "tcol", None))
    return jax.shard_map(body, mesh=mesh, in_specs=in_specs, out_specs=out_specs, check_vma=False)
```

```python
import math

import jax
import jax.numpy as jnp
import numpy as np
from jax import lax
from jax.experimental import pallas as pl
from jax.experimental.pallas import tpu as pltpu
from jax.sharding import PartitionSpec as P

PERIOD = 64
STEP_SIZE = 0.01
DRIVE_DEPTH = 0.5
MESH = pl.DeviceIdType.MESH
F32 = jnp.float32
BF16 = jnp.bfloat16

N = 16
TILE = 8
K = 512
BLOCK = K // N
LANES = N * TILE
WIDE = TILE * LANES
CELLS = TILE * TILE
NORM = 1.0 / math.sqrt(K)

NT = (((1,), (1,)), ((), ()))
NN = (((1,), (0,)), ((), ()))

SITE, MIRROR, INNER, SIGMA, GREEN_A, GREEN_B, OUT_B, OUT_A = range(8)


def mm(left, right, dims=NN):
    return lax.dot_general(left, right, dims, preferred_element_type=F32)


def block_swap(parts):
    parts = list(parts)
    lane = lax.broadcasted_iota(jnp.int32, parts[0].shape, 1)
    bit = 1
    while bit < N:
        shift = bit * TILE
        low = (lane // shift) % 2 == 0
        for i in range(N):
            if i & bit:
                continue
            first, second = parts[i], parts[i | bit]
            parts[i] = jnp.where(low, first, pltpu.roll(second, shift, 1))
            parts[i | bit] = jnp.where(low, pltpu.roll(first, LANES - shift, 1), second)
        bit *= 2
    return parts


def one_hot(hit):
    return jnp.where(hit, 1.0, 0.0).astype(BF16)


def kernel(
    offset_ref, map_hbm, lesser_hbm, greater_hbm, table_hbm, inner_hbm, outer_hbm,
    out_lesser, out_greater,
    momentum_map, green, table, inner, outer, perm, spread, own, mirror, selves,
    site_out, site_in, mirror_in, y_out, y_in, s_out, s_in,
    ga_out, ga_in, gb_out, gb_in, lefts, cb_out, cb_in, ca_out, ca_in,
    load_sems, send_sems, recv_sems,
):
    row = lax.axis_index("trow")
    col = lax.axis_index("tcol")
    barrier = pltpu.get_barrier_semaphore()

    def greet(step, carry):
        pl.semaphore_signal(
            barrier, inc=1, device_id=(lax.rem(row + step, N), col), device_id_type=MESH
        )
        pl.semaphore_signal(
            barrier, inc=1, device_id=(row, lax.rem(col + step, N)), device_id_type=MESH
        )
        return carry

    loads = [
        pltpu.make_async_copy(source, target, load_sems.at[i])
        for i, (source, target) in enumerate(
            (
                (map_hbm, momentum_map),
                (lesser_hbm, green.at[0]),
                (greater_hbm, green.at[1]),
                (table_hbm, table),
                (inner_hbm.at[row], inner),
                (outer_hbm, outer),
            )
        )
    ]
    for load in loads:
        load.start()
    lax.fori_loop(1, N, greet, 0)

    def row_copy(source, target, phase, other, slot):
        return pltpu.make_async_remote_copy(
            src_ref=source.at[other], dst_ref=target.at[slot],
            send_sem=send_sems.at[phase, other], recv_sem=recv_sems.at[phase, slot],
            device_id=(other, col), device_id_type=MESH,
        )

    def along_rows(source, target, phase):
        def one(step, carry):
            row_copy(source, target, phase, lax.rem(row + step, N), row).start()
            return carry

        lax.fori_loop(1, N, one, 0)
        target[pl.ds(row, 1)] = source[pl.ds(row, 1)]

    def rows_arrived(source, target, phase):
        def one(step, carry):
            other = lax.rem(row + N - step, N)
            row_copy(source, target, phase, other, other).wait_recv()
            return carry

        lax.fori_loop(1, N, one, 0)

    def rows_left(source, target, phase):
        def one(step, carry):
            row_copy(source, target, phase, lax.rem(row + step, N), row).wait_send()
            return carry

        lax.fori_loop(1, N, one, 0)

    plain = (lambda ref, i: ref.at[i], lambda ref, i: ref.at[i])
    to_window = (lambda ref, i: ref.at[i], lambda ref, i: ref.at[:, :, i])
    from_window = (lambda ref, i: ref.at[:, :, i], lambda ref, i: ref.at[i])

    def col_copy(source, target, phase, other, slot, form):
        return pltpu.make_async_remote_copy(
            src_ref=form[0](source, other), dst_ref=form[1](target, slot),
            send_sem=send_sems.at[phase, other], recv_sem=recv_sems.at[phase, slot],
            device_id=(row, other), device_id_type=MESH,
        )

    def along_cols(source, target, phase, form):
        def one(step, carry):
            col_copy(source, target, phase, lax.rem(col + step, N), col, form).start()
            return carry

        lax.fori_loop(1, N, one, 0)

    def cols_arrived(source, target, phase, form):
        def one(step, carry):
            other = lax.rem(col + N - step, N)
            col_copy(source, target, phase, other, other, form).wait_recv()
            return carry

        lax.fori_loop(1, N, one, 0)

    def cols_left(source, target, phase, form):
        def one(step, carry):
            col_copy(source, target, phase, lax.rem(col + step, N), col, form).wait_send()
            return carry

        lax.fori_loop(1, N, one, 0)

    place = lax.broadcasted_iota(jnp.int32, (K, 1), 0)
    loads[0].wait()
    perm[...] = one_hot((place // BLOCK) + N * (place % BLOCK) == momentum_map[...])
    r = lax.broadcasted_iota(jnp.int32, (LANES, LANES), 0)
    c = lax.broadcasted_iota(jnp.int32, (LANES, LANES), 1)
    swap = one_hot(
        (r // CELLS == c // CELLS)
        & ((r // TILE) % TILE == c % TILE)
        & (r % TILE == (c // TILE) % TILE)
    )

    for load in loads[1:]:
        load.wait()
    turned = []
    for half in range(2):
        natural = green[half].astype(F32).reshape(2 * CELLS, K).astype(BF16)
        turned.append(mm(swap, natural).astype(BF16))
        ordered = mm(turned[half], perm[...], NT)
        g_re, g_im = ordered[:CELLS], ordered[CELLS:]
        pairs = jnp.concatenate(
            [jnp.concatenate([g_re, -g_im], axis=1), jnp.concatenate([g_im, g_re], axis=1)],
            axis=0,
        ).astype(BF16)
        sites = mm(table[...], pairs, NT) * NORM
        site_out[:, half] = sites.reshape(N, BLOCK, LANES).astype(BF16)

    pl.semaphore_wait(barrier, 2 * (N - 1))
    along_rows(site_out, site_in, SITE)
    for half in range(2):
        spectral = mm(perm[...], turned[half], NT)
        ga_out[:, half] = spectral.reshape(N, BLOCK, LANES).astype(BF16)
    along_rows(ga_out, ga_in, GREEN_A)

    def pass_on(other):
        @pl.when(other != col)
        def _():
            col_copy(site_in, mirror_in, MIRROR, other, col, plain).start()

        @pl.when(other == col)
        def _():
            mirror_in[pl.ds(col, 1)] = site_in[pl.ds(col, 1)]

    pass_on(row)

    def relay(step, carry):
        other = lax.rem(row + N - step, N)
        row_copy(site_out, site_in, SITE, other, other).wait_recv()
        pass_on(other)
        return carry

    lax.fori_loop(1, N, relay, 0)

    for half in range(2):
        for part in range(2):
            base = part * 16
            swapped = block_swap(
                [site_in[a, half, base : base + 16, :].astype(F32) for a in range(N)]
            )
            for q in range(N):
                at, lane = (q // TILE) * BLOCK + base, (q % TILE) * LANES
                own[half, at : at + 16, lane : lane + LANES] = swapped[q].astype(BF16)

    rows_arrived(ga_out, ga_in, GREEN_A)
    for half in range(2):
        for part in range(2):
            base = part * 16
            swapped = block_swap(
                [ga_in[a, half, base : base + 16, :].astype(F32) for a in range(N)]
            )
            for q in range(N):
                start = (half * N + q) * BLOCK + base
                spread[start : start + 16, :] = swapped[q]
    for m in range(BLOCK):
        picked = spread[pl.ds(m, BLOCK, stride=BLOCK), :]
        gb_out[m // 2, m % 2] = picked.reshape(4, TILE, LANES).astype(BF16)
    along_cols(gb_out, gb_in, GREEN_B, to_window)
    gb_in[:, :, pl.ds(col, 1)] = gb_out[pl.ds(col, 1)].reshape(2, 4, 1, TILE, LANES)

    steps = lax.broadcasted_iota(jnp.int32, (TILE, LANES), 1)
    late = lax.broadcasted_iota(jnp.int32, (TILE, LANES), 0) + col * TILE

    def drive(at):
        phase = ((offset_ref[0] + at) % PERIOD).astype(F32) * (2.0 * math.pi / PERIOD)
        return 1.0 + DRIVE_DEPTH * jnp.cos(phase)

    product = drive(late) * drive(steps)
    coupling = jnp.concatenate([product[i : i + 1] for i in range(TILE)], axis=1)
    fr = lax.broadcasted_iota(jnp.int32, (2 * BLOCK, 2 * BLOCK), 0)
    fc = lax.broadcasted_iota(jnp.int32, (2 * BLOCK, 2 * BLOCK), 1)
    first_run = (fc // 16) % 2 == 0
    inside = fc + jnp.where(first_run, 16, -16)
    edge = (fc // 16) * 16 + jnp.where(first_run, (16 - fc % 16) % 16, 15 - fc % 16)
    flip = one_hot(fr == inside + jnp.where(row == 0, 1, 0) * (edge - inside))

    cols_arrived(site_in, mirror_in, MIRROR, plain)
    spread[...] = mm(mirror_in[...].reshape(2 * K, LANES), swap)
    for half in range(2):
        for part in range(2):
            base = part * 16
            swapped = block_swap(
                [
                    spread[pl.ds(b * 2 * BLOCK + half * BLOCK + base, 16), :]
                    for b in range(N)
                ]
            )
            for q in range(N):
                at, lane = (q // TILE) * BLOCK + base, (q % TILE) * LANES
                mirror[half, at : at + 16, lane : lane + LANES] = swapped[q].astype(BF16)
    for half in range(2):
        first_re, first_im = own[half, :BLOCK].astype(F32), own[half, BLOCK:].astype(F32)
        other = mm(flip, mirror[1 - half])
        other_re, other_im = other[:BLOCK], other[BLOCK:]
        square_re = first_re * first_re - first_im * first_im
        square_im = 2.0 * first_re * first_im
        self_re = coupling * (square_re * other_re - square_im * other_im)
        self_im = coupling * (square_re * other_im + square_im * other_re)
        at = half * 2 * BLOCK
        selves[at : at + BLOCK] = self_re.astype(BF16)
        selves[at + BLOCK : at + 2 * BLOCK] = self_im.astype(BF16)
    doubled = jnp.concatenate([selves[...], selves[...]], axis=0)
    y_out[...] = mm(inner[...], doubled).reshape(N, TILE, WIDE).astype(BF16)
    along_rows(y_out, y_in, INNER)

    down = lax.broadcasted_iota(jnp.int32, (LANES, LANES), 0)
    across = lax.broadcasted_iota(jnp.int32, (LANES, LANES), 1)
    cols_arrived(gb_out, gb_in, GREEN_B, to_window)
    for k in range(2):
        g = [gb_in[k, i].astype(F32).reshape(LANES, LANES) for i in range(4)]
        advanced = [jnp.where(across <= down, g[i] - g[2 + i], 0.0) for i in range(2)]
        for half in range(2):
            g_re, g_im = g[2 * half], g[2 * half + 1]
            for i, blocks in enumerate(
                ([g_re, -g_im, advanced[0], -advanced[1]], [g_im, g_re, advanced[1], advanced[0]])
            ):
                lefts[k, half, i * LANES : (i + 1) * LANES, :] = jnp.concatenate(
                    blocks, axis=1
                ).astype(BF16)

    rows_arrived(y_out, y_in, INNER)
    arrived = y_in[...].astype(F32).reshape(LANES, WIDE).astype(BF16)
    sigma = mm(outer[...], jnp.concatenate([arrived, arrived], axis=0)) * NORM
    s_out[...] = sigma.reshape(N, TILE, WIDE).astype(BF16)
    along_cols(s_out, s_in, SIGMA, plain)
    s_in[pl.ds(col, 1)] = s_out[pl.ds(col, 1)]
    cols_arrived(s_out, s_in, SIGMA, plain)
    for b in range(N):
        for t in range(TILE):
            start = (b * TILE + t) * TILE
            spread[start : start + TILE, :] = s_in[b, :, t * LANES : (t + 1) * LANES].astype(F32)
    for k in range(2):
        s = [spread[pl.ds(4 * k + i, LANES, stride=TILE), :] for i in range(4)]
        retarded = [jnp.where(down <= across, s[2 + i] - s[i], 0.0) for i in range(2)]
        for half in range(2):
            right = jnp.concatenate(
                retarded + [s[2 * half], s[2 * half + 1]], axis=0
            ).astype(BF16)
            total = mm(lefts[k, half], right) * STEP_SIZE
            total = total.reshape(2, N, TILE, LANES).astype(BF16)
            cb_out[k, 2 * half] = total[0]
            cb_out[k, 2 * half + 1] = total[1]
    along_cols(cb_out, cb_in, OUT_B, from_window)
    cb_in[pl.ds(col, 1)] = cb_out[:, :, pl.ds(col, 1)].reshape(1, 2, 4, TILE, LANES)
    cols_arrived(cb_out, cb_in, OUT_B, from_window)
    for m in range(BLOCK):
        spread[m * BLOCK : (m + 1) * BLOCK, :] = (
            cb_in[m // 2, m % 2].astype(F32).reshape(BLOCK, LANES)
        )
    for half in range(2):
        for part in range(2):
            base = part * 16
            swapped = block_swap(
                [
                    spread[pl.ds(base * BLOCK + half * N + q, 16, stride=BLOCK), :]
                    for q in range(N)
                ]
            )
            for a in range(N):
                ca_out[a, half, base : base + 16, :] = swapped[a].astype(BF16)
    along_rows(ca_out, ca_in, OUT_A)
    rows_arrived(ca_out, ca_in, OUT_A)
    for half, out in enumerate((out_lesser, out_greater)):
        full = ca_in[:, half].reshape(K, LANES)
        cells = mm(swap, full, NT).astype(BF16)
        out[...] = mm(cells, perm[...]).reshape(2, TILE, TILE, K).astype(BF16)

    def passed_on(step, carry):
        other = lax.rem(row + step, N)

        @pl.when(other != col)
        def _():
            col_copy(site_in, mirror_in, MIRROR, other, col, plain).wait_send()

        return carry

    lax.fori_loop(0, N, passed_on, 0)
    rows_left(site_out, site_in, SITE)
    rows_left(ga_out, ga_in, GREEN_A)
    cols_left(gb_out, gb_in, GREEN_B, to_window)
    rows_left(y_out, y_in, INNER)
    cols_left(s_out, s_in, SIGMA, plain)
    cols_left(cb_out, cb_in, OUT_B, from_window)
    rows_left(ca_out, ca_in, OUT_A)


def sites_of(block):
    run = 32 * np.arange(16)
    if block == 0:
        return np.concatenate([run, 16 + run])
    return np.concatenate([block + run, (-block - run) % K])


def split(matrix):
    high = matrix.astype(jnp.bfloat16)
    low = (matrix - high.astype(np.float64)).astype(jnp.bfloat16)
    return np.concatenate([high, low], axis=-1)


def inverse_block(angle):
    cos, sin = np.cos(angle), np.sin(angle)
    return np.stack([np.stack([cos, sin], -1), np.stack([-sin, cos], -1)], -2)


def constants():
    order = (np.arange(K) // BLOCK) + N * (np.arange(K) % BLOCK)
    sites = np.concatenate([sites_of(block) for block in range(N)])
    phases = (sites[:, None] * order[None, :] % K).astype(np.float32) * np.float32(
        2.0 * math.pi / K
    )
    table = np.concatenate([np.cos(phases), np.sin(phases)], axis=1).astype(jnp.bfloat16)
    inner = np.zeros((N, N, 2, 2, 2, 2, 2, 2, 16))
    for block in range(N):
        near = sites_of(block).reshape(2, 16)
        angle = 2.0 * math.pi / K * (np.arange(N)[:, None, None] * near[None] % K)
        turn = inverse_block(angle)
        for half in range(2):
            for run in range(2):
                inner[block, :, half, :, run, half, :, run, :] = turn[:, run].transpose(0, 2, 3, 1)
    residues = np.array([[0, 16]] + [[b, 32 - b] for b in range(1, N)])
    angle = 2.0 * math.pi / 32 * (np.arange(32)[:, None, None] * residues[None] % 32)
    turn = inverse_block(angle)
    outer = np.zeros((32, 2, 2, N, 2, 2, 2))
    for half in range(2):
        outer[:, half, :, :, half] = turn.transpose(0, 3, 1, 4, 2)
    return table, split(inner.reshape(N, LANES, LANES)), split(outer.reshape(LANES, LANES))


def body(green_lesser, green_greater, lattice_map, time_offset):
    hbm = pl.BlockSpec(memory_space=pltpu.MemorySpace.HBM)
    vmem = pl.BlockSpec(memory_space=pltpu.MemorySpace.VMEM)
    tile = jax.ShapeDtypeStruct((2, TILE, TILE, K), BF16)
    by_row = pltpu.VMEM((N, 2, BLOCK, LANES), BF16)
    by_col = pltpu.VMEM((N, 2, 4, TILE, LANES), BF16)
    wide = pltpu.VMEM((N, TILE, WIDE), BF16)
    window = pltpu.VMEM((2, 4, N, TILE, LANES), BF16)
    halves = pltpu.VMEM((2, 2 * BLOCK, WIDE), BF16)
    return pl.pallas_call(
        kernel,
        out_shape=(tile, tile),
        in_specs=[pl.BlockSpec(memory_space=pltpu.MemorySpace.SMEM)] + [hbm] * 6,
        out_specs=(vmem, vmem),
        scratch_shapes=[
            pltpu.VMEM((1, K), jnp.int32),
            pltpu.VMEM((2, 2, TILE, TILE, K), BF16),
            pltpu.VMEM((K, 2 * K), BF16),
            pltpu.VMEM((LANES, 2 * LANES), BF16),
            pltpu.VMEM((LANES, 2 * LANES), BF16),
            pltpu.VMEM((K, K), BF16),
            pltpu.VMEM((2 * K, LANES), F32),
            halves, halves,
            pltpu.VMEM((LANES, WIDE), BF16),
            by_row, by_row, by_row,
            wide, wide, wide, wide,
            by_row, by_row, by_col, window,
            pltpu.VMEM((2, 2, 2 * LANES, 4 * LANES), BF16),
            window, by_col, by_row, by_row,
            pltpu.SemaphoreType.DMA((6,)),
            pltpu.SemaphoreType.DMA((8, N)),
            pltpu.SemaphoreType.DMA((8, N)),
        ],
        compiler_params=pltpu.CompilerParams(
            collective_id=0, has_side_effects=True, vmem_limit_bytes=67_043_328
        ),
    )(
        time_offset, lattice_map.reshape(1, K), green_lesser, green_greater,
        *(jnp.asarray(value) for value in constants()),
    )


def solution(mesh):
    in_specs = (P(None, "trow", "tcol", None), P(None, "trow", "tcol", None), P(), P())
    out_specs = (P(None, "trow", "tcol", None), P(None, "trow", "tcol", None))
    return jax.shard_map(body, mesh=mesh, in_specs=in_specs, out_specs=out_specs, check_vma=False)
```

```python
import math

import jax
import jax.numpy as jnp
import numpy as np
from jax import lax
from jax.experimental import pallas as pl
from jax.experimental.pallas import tpu as pltpu
from jax.sharding import PartitionSpec as P

PERIOD = 64
STEP_SIZE = 0.01
DRIVE_DEPTH = 0.5
MESH = pl.DeviceIdType.MESH
F32 = jnp.float32
BF16 = jnp.bfloat16

N = 16
TILE = 8
K = 512
BLOCK = K // N
LANES = N * TILE
WIDE = TILE * LANES
CELLS = TILE * TILE
NORM = 1.0 / math.sqrt(K)

NT = (((1,), (1,)), ((), ()))
NN = (((1,), (0,)), ((), ()))

SITE, MIRROR, INNER, SIGMA, GREEN_A, GREEN_B = range(6)

ROW_OFFSETS = sorted(
    ((x, y, c) for x in (2, 1, -1, 0) for y in (1, 0) for c in (0, 1)),
    key=lambda o: -(abs(o[0]) + o[1] + 0.2 * o[2]),
)[:-1]
COL_OFFSETS = sorted(
    ((y, z) for z in (4, 3, -3, 2, -2, 1, -1, 0) for y in (1, 0)),
    key=lambda o: -(abs(o[1]) + 2 * o[0]),
)


def row_at(row, offset, sign=1):
    x, y, c = row // 4, (row // 2) % 2, row % 2
    dx, dy, dc = offset
    return ((x + sign * dx + 4) % 4) * 4 + ((y + dy) % 2) * 2 + (c + dc) % 2


def col_at(col, offset, sign=1):
    y, z = col // 8, col % 8
    dy, dz = offset
    return ((y + dy) % 2) * 8 + (z + sign * dz + 8) % 8


def mm(left, right, dims=NN):
    return lax.dot_general(left, right, dims, preferred_element_type=F32)


def block_swap(parts):
    parts = list(parts)
    lane = lax.broadcasted_iota(jnp.int32, parts[0].shape, 1)
    bit = 1
    while bit < N:
        shift = bit * TILE
        low = (lane // shift) % 2 == 0
        for i in range(N):
            if i & bit:
                continue
            first, second = parts[i], parts[i | bit]
            parts[i] = jnp.where(low, first, pltpu.roll(second, shift, 1))
            parts[i | bit] = jnp.where(low, pltpu.roll(first, LANES - shift, 1), second)
        bit *= 2
    return parts


def one_hot(hit):
    return jnp.where(hit, 1.0, 0.0).astype(BF16)


def kernel(
    offset_ref, map_hbm, lesser_hbm, greater_hbm, table_hbm, inner_hbm, outer_hbm,
    out_lesser, out_greater,
    momentum_map, green, table, inner, outer, perm, spread, own, mirror, selves,
    site_out, site_in, mirror_in, y_out, y_in, s_out, s_in,
    ga_out, ga_in, gb_out, gb_in, lefts, results, select, x_out, x_in,
    load_sems, send_sems, recv_sems, tile_sems,
):
    row = lax.axis_index("trow")
    col = lax.axis_index("tcol")
    barrier = pltpu.get_barrier_semaphore()

    loads = [
        pltpu.make_async_copy(source, target, load_sems.at[i])
        for i, (source, target) in enumerate(
            (
                (map_hbm, momentum_map),
                (lesser_hbm, green.at[0]),
                (greater_hbm, green.at[1]),
                (table_hbm, table),
                (inner_hbm.at[row], inner),
                (outer_hbm, outer),
            )
        )
    ]
    for load in loads:
        load.start()
    for offset in COL_OFFSETS[:-1]:
        pl.semaphore_signal(
            barrier, inc=1, device_id=(row, col_at(col, offset)), device_id_type=MESH
        )
    for offset in ROW_OFFSETS:
        pl.semaphore_signal(
            barrier, inc=1, device_id=(row_at(row, offset), col), device_id_type=MESH
        )

    def row_copy(source, target, phase, other, slot):
        return pltpu.make_async_remote_copy(
            src_ref=source.at[other], dst_ref=target.at[slot],
            send_sem=send_sems.at[phase, other], recv_sem=recv_sems.at[phase, slot],
            device_id=(other, col), device_id_type=MESH,
        )

    def along_rows(source, target, phase):
        for offset in ROW_OFFSETS:
            row_copy(source, target, phase, row_at(row, offset), row).start()
        target[pl.ds(row, 1)] = source[pl.ds(row, 1)]

    def rows_arrived(source, target, phase):
        for offset in ROW_OFFSETS:
            other = row_at(row, offset, -1)
            row_copy(source, target, phase, other, other).wait_recv()

    def rows_left(source, target, phase):
        for offset in ROW_OFFSETS:
            row_copy(source, target, phase, row_at(row, offset), row).wait_send()

    plain = (lambda ref, i: ref.at[i], lambda ref, i: ref.at[i])
    to_window = (lambda ref, i: ref.at[i], lambda ref, i: ref.at[:, :, i])

    def col_copy(source, target, phase, other, slot, form):
        return pltpu.make_async_remote_copy(
            src_ref=form[0](source, other), dst_ref=form[1](target, slot),
            send_sem=send_sems.at[phase, other], recv_sem=recv_sems.at[phase, slot],
            device_id=(row, other), device_id_type=MESH,
        )

    def along_cols(source, target, phase, form):
        for offset in COL_OFFSETS[:-1]:
            col_copy(source, target, phase, col_at(col, offset), col, form).start()

    def cols_arrived(source, target, phase, form):
        for offset in COL_OFFSETS[:-1]:
            other = col_at(col, offset, -1)
            col_copy(source, target, phase, other, other, form).wait_recv()

    def cols_left(source, target, phase, form):
        for offset in COL_OFFSETS[:-1]:
            col_copy(source, target, phase, col_at(col, offset), col, form).wait_send()

    place = lax.broadcasted_iota(jnp.int32, (K, 1), 0)
    loads[0].wait()
    perm[...] = one_hot((place // BLOCK) + N * (place % BLOCK) == momentum_map[...])
    r = lax.broadcasted_iota(jnp.int32, (LANES, LANES), 0)
    c = lax.broadcasted_iota(jnp.int32, (LANES, LANES), 1)
    swap = one_hot(
        (r // CELLS == c // CELLS)
        & ((r // TILE) % TILE == c % TILE)
        & (r % TILE == (c // TILE) % TILE)
    )

    for load in loads[1:]:
        load.wait()
    turned = []
    for half in range(2):
        natural = green[half].astype(F32).reshape(2 * CELLS, K).astype(BF16)
        turned.append(mm(swap, natural).astype(BF16))
        ordered = mm(turned[half], perm[...], NT)
        g_re, g_im = ordered[:CELLS], ordered[CELLS:]
        pairs = jnp.concatenate(
            [jnp.concatenate([g_re, -g_im], axis=1), jnp.concatenate([g_im, g_re], axis=1)],
            axis=0,
        ).astype(BF16)
        sites = mm(table[...], pairs, NT) * NORM
        site_out[:, half] = sites.reshape(N, BLOCK, LANES).astype(BF16)

    pl.semaphore_wait(barrier, 2 * (N - 1))
    along_rows(site_out, site_in, SITE)
    for half in range(2):
        spectral = mm(perm[...], turned[half], NT)
        ga_out[:, half] = spectral.reshape(N, BLOCK, LANES).astype(BF16)
    along_rows(ga_out, ga_in, GREEN_A)

    def pass_on(other):
        @pl.when(other != col)
        def _():
            col_copy(site_in, mirror_in, MIRROR, other, col, plain).start()

        @pl.when(other == col)
        def _():
            mirror_in[pl.ds(col, 1)] = site_in[pl.ds(col, 1)]

    pass_on(row)

    for offset in ROW_OFFSETS:
        other = row_at(row, offset, -1)
        row_copy(site_out, site_in, SITE, other, other).wait_recv()
        pass_on(other)

    for half in range(2):
        for part in range(2):
            base = part * 16
            swapped = block_swap(
                [site_in[a, half, base : base + 16, :].astype(F32) for a in range(N)]
            )
            for q in range(N):
                at, lane = (q // TILE) * BLOCK + base, (q % TILE) * LANES
                own[half, at : at + 16, lane : lane + LANES] = swapped[q].astype(BF16)

    rows_arrived(ga_out, ga_in, GREEN_A)
    for half in range(2):
        for part in range(2):
            base = part * 16
            swapped = block_swap(
                [ga_in[a, half, base : base + 16, :].astype(F32) for a in range(N)]
            )
            for q in range(N):
                start = (half * N + q) * BLOCK + base
                spread[start : start + 16, :] = swapped[q]
    for m in range(BLOCK):
        picked = spread[pl.ds(m, BLOCK, stride=BLOCK), :]
        gb_out[m // 2, m % 2] = picked.reshape(4, TILE, LANES).astype(BF16)
    along_cols(gb_out, gb_in, GREEN_B, to_window)
    gb_in[:, :, pl.ds(col, 1)] = gb_out[pl.ds(col, 1)].reshape(2, 4, 1, TILE, LANES)

    steps = lax.broadcasted_iota(jnp.int32, (TILE, LANES), 1)
    late = lax.broadcasted_iota(jnp.int32, (TILE, LANES), 0) + col * TILE

    def drive(at):
        phase = ((offset_ref[0] + at) % PERIOD).astype(F32) * (2.0 * math.pi / PERIOD)
        return 1.0 + DRIVE_DEPTH * jnp.cos(phase)

    product = drive(late) * drive(steps)
    coupling = jnp.concatenate([product[i : i + 1] for i in range(TILE)], axis=1)
    fr = lax.broadcasted_iota(jnp.int32, (2 * BLOCK, 2 * BLOCK), 0)
    fc = lax.broadcasted_iota(jnp.int32, (2 * BLOCK, 2 * BLOCK), 1)
    first_run = (fc // 16) % 2 == 0
    inside = fc + jnp.where(first_run, 16, -16)
    edge = (fc // 16) * 16 + jnp.where(first_run, (16 - fc % 16) % 16, 15 - fc % 16)
    flip = one_hot(fr == inside + jnp.where(row == 0, 1, 0) * (edge - inside))

    cols_arrived(site_in, mirror_in, MIRROR, plain)
    spread[...] = mm(mirror_in[...].reshape(2 * K, LANES), swap)
    for half in range(2):
        for part in range(2):
            base = part * 16
            swapped = block_swap(
                [
                    spread[pl.ds(b * 2 * BLOCK + half * BLOCK + base, 16), :]
                    for b in range(N)
                ]
            )
            for q in range(N):
                at, lane = (q // TILE) * BLOCK + base, (q % TILE) * LANES
                mirror[half, at : at + 16, lane : lane + LANES] = swapped[q].astype(BF16)
    for half in range(2):
        first_re, first_im = own[half, :BLOCK].astype(F32), own[half, BLOCK:].astype(F32)
        other = mm(flip, mirror[1 - half])
        other_re, other_im = other[:BLOCK], other[BLOCK:]
        square_re = first_re * first_re - first_im * first_im
        square_im = 2.0 * first_re * first_im
        self_re = coupling * (square_re * other_re - square_im * other_im)
        self_im = coupling * (square_re * other_im + square_im * other_re)
        at = half * 2 * BLOCK
        selves[at : at + BLOCK] = self_re.astype(BF16)
        selves[at + BLOCK : at + 2 * BLOCK] = self_im.astype(BF16)
    doubled = jnp.concatenate([selves[...], selves[...]], axis=0)
    y_out[...] = mm(inner[...], doubled).reshape(N, TILE, WIDE).astype(BF16)
    along_rows(y_out, y_in, INNER)

    down = lax.broadcasted_iota(jnp.int32, (LANES, LANES), 0)
    across = lax.broadcasted_iota(jnp.int32, (LANES, LANES), 1)
    cols_arrived(gb_out, gb_in, GREEN_B, to_window)
    for k in range(2):
        g = [gb_in[k, i].astype(F32).reshape(LANES, LANES) for i in range(4)]
        advanced = [jnp.where(across <= down, g[i] - g[2 + i], 0.0) for i in range(2)]
        for half in range(2):
            g_re, g_im = g[2 * half], g[2 * half + 1]
            for i, blocks in enumerate(
                ([g_re, -g_im, advanced[0], -advanced[1]], [g_im, g_re, advanced[1], advanced[0]])
            ):
                lefts[k, half, i * LANES : (i + 1) * LANES, :] = jnp.concatenate(
                    blocks, axis=1
                ).astype(BF16)

    rows_arrived(y_out, y_in, INNER)
    arrived = y_in[...].astype(F32).reshape(LANES, WIDE).astype(BF16)
    sigma = mm(outer[...], jnp.concatenate([arrived, arrived], axis=0)) * NORM
    s_out[...] = sigma.reshape(N, TILE, WIDE).astype(BF16)
    along_cols(s_out, s_in, SIGMA, plain)
    s_in[pl.ds(col, 1)] = s_out[pl.ds(col, 1)]
    cols_arrived(s_out, s_in, SIGMA, plain)
    for b in range(N):
        for t in range(TILE):
            start = (b * TILE + t) * TILE
            spread[start : start + TILE, :] = s_in[b, :, t * LANES : (t + 1) * LANES].astype(F32)
    for k in range(2):
        s = [spread[pl.ds(4 * k + i, LANES, stride=TILE), :] for i in range(4)]
        retarded = [jnp.where(down <= across, s[2 + i] - s[i], 0.0) for i in range(2)]
        for half in range(2):
            right = jnp.concatenate(
                retarded + [s[2 * half], s[2 * half + 1]], axis=0
            ).astype(BF16)
            total = mm(lefts[k, half], right) * STEP_SIZE
            start = (4 * k + 2 * half) * LANES
            results[start : start + 2 * LANES, :] = total

    for piece in range(4):
        swapped = block_swap(
            [
                results[pl.ds((q // 2) * LANES + q % 2 + 32 * piece, 16, stride=2), :]
                for q in range(N)
            ]
        )
        for a in range(N):
            start = a * N + 4 * piece
            x_out[start : start + 4] = swapped[a].reshape(4, 4, LANES).astype(BF16)
    me = row * N + col

    def tile_copy(other_row, other_col):
        return pltpu.make_async_remote_copy(
            src_ref=x_out.at[other_row * N + other_col], dst_ref=x_in.at[me],
            send_sem=tile_sems.at[0], recv_sem=tile_sems.at[1],
            device_id=(other_row, other_col), device_id_type=MESH,
        )

    for offset in COL_OFFSETS:
        other_col = col_at(col, offset)

        def one(i, carry, other_col=other_col):
            quarter = i // 4
            dx = jnp.where(quarter == 0, 2, jnp.where(quarter == 3, 0, 2 * quarter - 1))
            other_row = (
                ((row // 4 + dx) % 4) * 4
                + ((row // 2 + 1 - (i // 2) % 2) % 2) * 2
                + (row + 1 - i % 2) % 2
            )
            tile_copy(other_row, other_col).start()
            return carry

        lax.fori_loop(0, N - (1 if offset == (0, 0) else 0), one, 0)
    x_in[pl.ds(me, 1)] = x_out[pl.ds(me, 1)]

    place = lax.broadcasted_iota(jnp.int32, (K, 1), 0)
    member, device = place // (N * N), place % (N * N)
    perm[...] = one_hot(
        device // N + N * (2 * (device % N) + member) == momentum_map[...]
    )
    part, early, late = (place // CELLS) % 4, (place // TILE) % TILE, place % TILE
    lane = (late // 2) * LANES + ((member * 4 + part) * 2 + late % 2) * TILE + early
    select[...] = one_hot(lane == lax.broadcasted_iota(jnp.int32, (1, K), 1))
    everyone = pl.ds(0, N * N - 1)
    pltpu.make_async_copy(x_in.at[everyone], x_in.at[everyone], tile_sems.at[1]).wait()
    for d in range(N * N):
        spread[4 * d : 4 * d + 4, :] = x_in[d].astype(F32)
    rows = jnp.concatenate(
        [spread[pl.ds(i, N * N, stride=4), :] for i in range(4)], axis=1
    ).astype(BF16)
    cells = mm(select[...], rows, NT).astype(BF16)
    cells = jnp.concatenate([cells[: K // 2], cells[K // 2 :]], axis=1)
    final = mm(cells, perm[...]).astype(BF16)
    for half, out in enumerate((out_lesser, out_greater)):
        out[...] = (
            final[half * 2 * CELLS : (half + 1) * 2 * CELLS]
            .astype(F32)
            .reshape(2, TILE, TILE, K)
            .astype(BF16)
        )
    pltpu.make_async_copy(x_out.at[everyone], x_out.at[everyone], tile_sems.at[0]).wait()

    def passed_on(step, carry):
        other = lax.rem(row + step, N)

        @pl.when(other != col)
        def _():
            col_copy(site_in, mirror_in, MIRROR, other, col, plain).wait_send()

        return carry

    lax.fori_loop(0, N, passed_on, 0)
    rows_left(site_out, site_in, SITE)
    rows_left(ga_out, ga_in, GREEN_A)
    cols_left(gb_out, gb_in, GREEN_B, to_window)
    rows_left(y_out, y_in, INNER)
    cols_left(s_out, s_in, SIGMA, plain)


def sites_of(block):
    run = 32 * np.arange(16)
    if block == 0:
        return np.concatenate([run, 16 + run])
    return np.concatenate([block + run, (-block - run) % K])


def split(matrix):
    high = matrix.astype(jnp.bfloat16)
    low = (matrix - high.astype(np.float64)).astype(jnp.bfloat16)
    return np.concatenate([high, low], axis=-1)


def inverse_block(angle):
    cos, sin = np.cos(angle), np.sin(angle)
    return np.stack([np.stack([cos, sin], -1), np.stack([-sin, cos], -1)], -2)


def constants():
    order = (np.arange(K) // BLOCK) + N * (np.arange(K) % BLOCK)
    sites = np.concatenate([sites_of(block) for block in range(N)])
    phases = (sites[:, None] * order[None, :] % K).astype(np.float32) * np.float32(
        2.0 * math.pi / K
    )
    table = np.concatenate([np.cos(phases), np.sin(phases)], axis=1).astype(jnp.bfloat16)
    inner = np.zeros((N, N, 2, 2, 2, 2, 2, 2, 16))
    for block in range(N):
        near = sites_of(block).reshape(2, 16)
        angle = 2.0 * math.pi / K * (np.arange(N)[:, None, None] * near[None] % K)
        turn = inverse_block(angle)
        for half in range(2):
            for run in range(2):
                inner[block, :, half, :, run, half, :, run, :] = turn[:, run].transpose(0, 2, 3, 1)
    residues = np.array([[0, 16]] + [[b, 32 - b] for b in range(1, N)])
    angle = 2.0 * math.pi / 32 * (np.arange(32)[:, None, None] * residues[None] % 32)
    turn = inverse_block(angle)
    outer = np.zeros((32, 2, 2, N, 2, 2, 2))
    for half in range(2):
        outer[:, half, :, :, half] = turn.transpose(0, 3, 1, 4, 2)
    return table, split(inner.reshape(N, LANES, LANES)), split(outer.reshape(LANES, LANES))


def body(green_lesser, green_greater, lattice_map, time_offset):
    hbm = pl.BlockSpec(memory_space=pltpu.MemorySpace.HBM)
    vmem = pl.BlockSpec(memory_space=pltpu.MemorySpace.VMEM)
    tile = jax.ShapeDtypeStruct((2, TILE, TILE, K), BF16)
    by_row = pltpu.VMEM((N, 2, BLOCK, LANES), BF16)
    by_col = pltpu.VMEM((N, 2, 4, TILE, LANES), BF16)
    wide = pltpu.VMEM((N, TILE, WIDE), BF16)
    window = pltpu.VMEM((2, 4, N, TILE, LANES), BF16)
    halves = pltpu.VMEM((2, 2 * BLOCK, WIDE), BF16)
    return pl.pallas_call(
        kernel,
        out_shape=(tile, tile),
        in_specs=[pl.BlockSpec(memory_space=pltpu.MemorySpace.SMEM)] + [hbm] * 6,
        out_specs=(vmem, vmem),
        scratch_shapes=[
            pltpu.VMEM((1, K), jnp.int32),
            pltpu.VMEM((2, 2, TILE, TILE, K), BF16),
            pltpu.VMEM((K, 2 * K), BF16),
            pltpu.VMEM((LANES, 2 * LANES), BF16),
            pltpu.VMEM((LANES, 2 * LANES), BF16),
            pltpu.VMEM((K, K), BF16),
            pltpu.VMEM((2 * K, LANES), F32),
            halves, halves,
            pltpu.VMEM((LANES, WIDE), BF16),
            by_row, by_row, by_row,
            wide, wide, wide, wide,
            by_row, by_row, by_col, window,
            pltpu.VMEM((2, 2, 2 * LANES, 4 * LANES), BF16),
            pltpu.VMEM((2 * K, LANES), F32),
            pltpu.VMEM((K, K), BF16),
            pltpu.VMEM((N * N, 4, LANES), BF16),
            pltpu.VMEM((N * N, 4, LANES), BF16),
            pltpu.SemaphoreType.DMA((6,)),
            pltpu.SemaphoreType.DMA((6, N)),
            pltpu.SemaphoreType.DMA((6, N)),
            pltpu.SemaphoreType.DMA((2,)),
        ],
        compiler_params=pltpu.CompilerParams(
            collective_id=0, has_side_effects=True, vmem_limit_bytes=67_043_328
        ),
    )(
        time_offset, lattice_map.reshape(1, K), green_lesser, green_greater,
        *(jnp.asarray(value) for value in constants()),
    )


def solution(mesh):
    in_specs = (P(None, "trow", "tcol", None), P(None, "trow", "tcol", None), P(), P())
    out_specs = (P(None, "trow", "tcol", None), P(None, "trow", "tcol", None))
    return jax.shard_map(body, mesh=mesh, in_specs=in_specs, out_specs=out_specs, check_vma=False)
```

```python
import math

import jax
import jax.numpy as jnp
import numpy as np
from jax import lax
from jax.experimental import pallas as pl
from jax.experimental.pallas import tpu as pltpu
from jax.sharding import PartitionSpec as P

PERIOD = 64
STEP_SIZE = 0.01
DRIVE_DEPTH = 0.5
MESH = pl.DeviceIdType.MESH
F32 = jnp.float32
BF16 = jnp.bfloat16

N = 16
TILE = 8
K = 512
BLOCK = K // N
LANES = N * TILE
WIDE = TILE * LANES
CELLS = TILE * TILE
NORM = 1.0 / math.sqrt(K)

NT = (((1,), (1,)), ((), ()))
NN = (((1,), (0,)), ((), ()))

SITE, MIRROR, INNER, SIGMA, GREEN_A, GREEN_B = range(6)

ROW_OFFSETS = sorted(
    ((x, y, c) for x in (2, 1, -1, 0) for y in (1, 0) for c in (0, 1)),
    key=lambda o: -(abs(o[0]) + o[1] + 0.2 * o[2]),
)[:-1]
COL_OFFSETS = sorted(
    ((y, z) for z in (4, 3, -3, 2, -2, 1, -1, 0) for y in (1, 0)),
    key=lambda o: -(abs(o[1]) + 2 * o[0]),
)


def row_at(row, offset, sign=1):
    x, y, c = row // 4, (row // 2) % 2, row % 2
    dx, dy, dc = offset
    return ((x + sign * dx + 4) % 4) * 4 + ((y + dy) % 2) * 2 + (c + dc) % 2


def col_at(col, offset, sign=1):
    y, z = col // 8, col % 8
    dy, dz = offset
    return ((y + dy) % 2) * 8 + (z + sign * dz + 8) % 8


def mm(left, right, dims=NN):
    return lax.dot_general(left, right, dims, preferred_element_type=F32)


def block_swap(parts):
    parts = list(parts)
    lane = lax.broadcasted_iota(jnp.int32, parts[0].shape, 1)
    bit = 1
    while bit < N:
        shift = bit * TILE
        low = (lane // shift) % 2 == 0
        for i in range(N):
            if i & bit:
                continue
            first, second = parts[i], parts[i | bit]
            parts[i] = jnp.where(low, first, pltpu.roll(second, shift, 1))
            parts[i | bit] = jnp.where(low, pltpu.roll(first, LANES - shift, 1), second)
        bit *= 2
    return parts


def one_hot(hit):
    return jnp.where(hit, 1.0, 0.0).astype(BF16)


def kernel(
    offset_ref, map_hbm, lesser_hbm, greater_hbm, table_hbm, inner_hbm, outer_hbm,
    out_lesser, out_greater,
    momentum_map, green, table, inner, outer, perm, spread, own, mirror, selves,
    site_out, site_in, mirror_in, y_out, y_in, s_out, s_in,
    ga_out, ga_in, gb_out, gb_in, lefts, results, select, x_out, x_in,
    load_sems, send_sems, recv_sems, tile_sems,
):
    row = lax.axis_index("trow")
    col = lax.axis_index("tcol")
    barrier = pltpu.get_barrier_semaphore()

    loads = [
        pltpu.make_async_copy(source, target, load_sems.at[i])
        for i, (source, target) in enumerate(
            (
                (map_hbm, momentum_map),
                (lesser_hbm, green.at[0]),
                (greater_hbm, green.at[1]),
                (table_hbm, table),
                (outer_hbm, outer),
                (inner_hbm.at[row], inner),
            )
        )
    ]
    for load in loads:
        load.start()
    for offset in COL_OFFSETS[:-1]:
        pl.semaphore_signal(
            barrier, inc=1, device_id=(row, col_at(col, offset)), device_id_type=MESH
        )
    for offset in ROW_OFFSETS:
        pl.semaphore_signal(
            barrier, inc=1, device_id=(row_at(row, offset), col), device_id_type=MESH
        )

    def row_copy(source, target, phase, other, slot):
        return pltpu.make_async_remote_copy(
            src_ref=source.at[other], dst_ref=target.at[slot],
            send_sem=send_sems.at[phase, other], recv_sem=recv_sems.at[phase, slot],
            device_id=(other, col), device_id_type=MESH,
        )

    def along_rows(source, target, phase):
        for offset in ROW_OFFSETS:
            row_copy(source, target, phase, row_at(row, offset), row).start()
        target[pl.ds(row, 1)] = source[pl.ds(row, 1)]

    def rows_arrived(source, target, phase):
        for offset in ROW_OFFSETS:
            other = row_at(row, offset, -1)
            row_copy(source, target, phase, other, other).wait_recv()

    def rows_left(source, target, phase):
        for offset in ROW_OFFSETS:
            row_copy(source, target, phase, row_at(row, offset), row).wait_send()

    plain = (lambda ref, i: ref.at[i], lambda ref, i: ref.at[i])
    to_window = (lambda ref, i: ref.at[i], lambda ref, i: ref.at[:, :, i])

    def col_copy(source, target, phase, other, slot, form):
        return pltpu.make_async_remote_copy(
            src_ref=form[0](source, other), dst_ref=form[1](target, slot),
            send_sem=send_sems.at[phase, other], recv_sem=recv_sems.at[phase, slot],
            device_id=(row, other), device_id_type=MESH,
        )

    def along_cols(source, target, phase, form):
        for offset in COL_OFFSETS[:-1]:
            col_copy(source, target, phase, col_at(col, offset), col, form).start()

    def cols_arrived(source, target, phase, form):
        for offset in COL_OFFSETS[:-1]:
            other = col_at(col, offset, -1)
            col_copy(source, target, phase, other, other, form).wait_recv()

    def cols_left(source, target, phase, form):
        for offset in COL_OFFSETS[:-1]:
            col_copy(source, target, phase, col_at(col, offset), col, form).wait_send()

    place = lax.broadcasted_iota(jnp.int32, (K, 1), 0)
    loads[0].wait()
    perm[...] = one_hot((place // BLOCK) + N * (place % BLOCK) == momentum_map[...])
    r = lax.broadcasted_iota(jnp.int32, (LANES, LANES), 0)
    c = lax.broadcasted_iota(jnp.int32, (LANES, LANES), 1)
    swap = one_hot(
        (r // CELLS == c // CELLS)
        & ((r // TILE) % TILE == c % TILE)
        & (r % TILE == (c // TILE) % TILE)
    )

    loads[1].wait()
    loads[2].wait()
    turned = []
    pairs = []
    for half in range(2):
        natural = green[half].astype(F32).reshape(2 * CELLS, K).astype(BF16)
        turned.append(mm(swap, natural).astype(BF16))
    turned = jnp.concatenate(turned, axis=0)
    ordered = mm(turned, perm[...], NT)
    for half in range(2):
        g_re = ordered[2 * half * CELLS : (2 * half + 1) * CELLS]
        g_im = ordered[(2 * half + 1) * CELLS : (2 * half + 2) * CELLS]
        pairs.append(jnp.concatenate([g_re, -g_im], axis=1))
        pairs.append(jnp.concatenate([g_im, g_re], axis=1))
    pairs = jnp.concatenate(pairs, axis=0).astype(BF16)
    loads[3].wait()
    sites = mm(table[...], pairs, NT) * NORM
    for half in range(2):
        site_out[:, half] = (
            sites[:, half * LANES : (half + 1) * LANES].reshape(N, BLOCK, LANES).astype(BF16)
        )

    pl.semaphore_wait(barrier, 2 * (N - 1))
    along_rows(site_out, site_in, SITE)
    spectral = mm(perm[...], turned, NT)
    for half in range(2):
        ga_out[:, half] = (
            spectral[:, half * LANES : (half + 1) * LANES].reshape(N, BLOCK, LANES).astype(BF16)
        )

    def pass_on(other):
        @pl.when(other != col)
        def _():
            col_copy(site_in, mirror_in, MIRROR, other, col, plain).start()

        @pl.when(other == col)
        def _():
            mirror_in[pl.ds(col, 1)] = site_in[pl.ds(col, 1)]

    pass_on(row)

    for offset in ROW_OFFSETS:
        other = row_at(row, offset, -1)
        row_copy(site_out, site_in, SITE, other, other).wait_recv()
        pass_on(other)
    along_rows(ga_out, ga_in, GREEN_A)

    for half in range(2):
        for part in range(2):
            base = part * 16
            swapped = block_swap(
                [site_in[a, half, base : base + 16, :].astype(F32) for a in range(N)]
            )
            for q in range(N):
                at, lane = (q // TILE) * BLOCK + base, (q % TILE) * LANES
                own[half, at : at + 16, lane : lane + LANES] = swapped[q].astype(BF16)

    rows_arrived(ga_out, ga_in, GREEN_A)
    for half in range(2):
        for part in range(2):
            base = part * 16
            swapped = block_swap(
                [ga_in[a, half, base : base + 16, :].astype(F32) for a in range(N)]
            )
            for q in range(N):
                start = (half * N + q) * BLOCK + base
                spread[start : start + 16, :] = swapped[q]
    for m in range(BLOCK):
        picked = spread[pl.ds(m, BLOCK, stride=BLOCK), :]
        gb_out[m // 2, m % 2] = picked.reshape(4, TILE, LANES).astype(BF16)
    gb_in[:, :, pl.ds(col, 1)] = gb_out[pl.ds(col, 1)].reshape(2, 4, 1, TILE, LANES)

    steps = lax.broadcasted_iota(jnp.int32, (TILE, LANES), 1)
    late = lax.broadcasted_iota(jnp.int32, (TILE, LANES), 0) + col * TILE

    def drive(at):
        phase = ((offset_ref[0] + at) % PERIOD).astype(F32) * (2.0 * math.pi / PERIOD)
        return 1.0 + DRIVE_DEPTH * jnp.cos(phase)

    product = drive(late) * drive(steps)
    coupling = jnp.concatenate([product[i : i + 1] for i in range(TILE)], axis=1)
    fr = lax.broadcasted_iota(jnp.int32, (2 * BLOCK, 2 * BLOCK), 0)
    fc = lax.broadcasted_iota(jnp.int32, (2 * BLOCK, 2 * BLOCK), 1)
    first_run = (fc // 16) % 2 == 0
    inside = fc + jnp.where(first_run, 16, -16)
    edge = (fc // 16) * 16 + jnp.where(first_run, (16 - fc % 16) % 16, 15 - fc % 16)
    flip = one_hot(fr == inside + jnp.where(row == 0, 1, 0) * (edge - inside))

    along_cols(gb_out, gb_in, GREEN_B, to_window)
    cols_arrived(site_in, mirror_in, MIRROR, plain)
    spread[...] = mm(mirror_in[...].reshape(2 * K, LANES), swap)
    for half in range(2):
        for part in range(2):
            base = part * 16
            swapped = block_swap(
                [
                    spread[pl.ds(b * 2 * BLOCK + half * BLOCK + base, 16), :]
                    for b in range(N)
                ]
            )
            for q in range(N):
                at, lane = (q // TILE) * BLOCK + base, (q % TILE) * LANES
                mirror[half, at : at + 16, lane : lane + LANES] = swapped[q].astype(BF16)
    for half in range(2):
        first_re, first_im = own[half, :BLOCK].astype(F32), own[half, BLOCK:].astype(F32)
        other = mm(flip, mirror[1 - half])
        other_re, other_im = other[:BLOCK], other[BLOCK:]
        square_re = first_re * first_re - first_im * first_im
        square_im = 2.0 * first_re * first_im
        self_re = coupling * (square_re * other_re - square_im * other_im)
        self_im = coupling * (square_re * other_im + square_im * other_re)
        at = half * 2 * BLOCK
        selves[at : at + BLOCK] = self_re.astype(BF16)
        selves[at + BLOCK : at + 2 * BLOCK] = self_im.astype(BF16)
    doubled = jnp.concatenate([selves[...], selves[...]], axis=0)
    loads[5].wait()
    y_out[...] = mm(inner[...], doubled).reshape(N, TILE, WIDE).astype(BF16)
    along_rows(y_out, y_in, INNER)

    down = lax.broadcasted_iota(jnp.int32, (LANES, LANES), 0)
    across = lax.broadcasted_iota(jnp.int32, (LANES, LANES), 1)
    cols_arrived(gb_out, gb_in, GREEN_B, to_window)
    for k in range(2):
        g = [gb_in[k, i].astype(F32).reshape(LANES, LANES) for i in range(4)]
        advanced = [jnp.where(across <= down, g[i] - g[2 + i], 0.0) for i in range(2)]
        for half in range(2):
            g_re, g_im = g[2 * half], g[2 * half + 1]
            for i, blocks in enumerate(
                ([g_re, -g_im, advanced[0], -advanced[1]], [g_im, g_re, advanced[1], advanced[0]])
            ):
                lefts[k, half, i * LANES : (i + 1) * LANES, :] = jnp.concatenate(
                    blocks, axis=1
                ).astype(BF16)

    loads[4].wait()
    rows_arrived(y_out, y_in, INNER)
    arrived = y_in[...].astype(F32).reshape(LANES, WIDE).astype(BF16)
    sigma = mm(outer[...], jnp.concatenate([arrived, arrived], axis=0)) * NORM
    s_out[...] = sigma.reshape(N, TILE, WIDE).astype(BF16)
    along_cols(s_out, s_in, SIGMA, plain)
    s_in[pl.ds(col, 1)] = s_out[pl.ds(col, 1)]
    cols_arrived(s_out, s_in, SIGMA, plain)
    for b in range(N):
        for t in range(TILE):
            start = (b * TILE + t) * TILE
            spread[start : start + TILE, :] = s_in[b, :, t * LANES : (t + 1) * LANES].astype(F32)
    for k in range(2):
        s = [spread[pl.ds(4 * k + i, LANES, stride=TILE), :] for i in range(4)]
        retarded = [jnp.where(down <= across, s[2 + i] - s[i], 0.0) for i in range(2)]
        for half in range(2):
            right = jnp.concatenate(
                retarded + [s[2 * half], s[2 * half + 1]], axis=0
            ).astype(BF16)
            total = mm(lefts[k, half], right) * STEP_SIZE
            start = (4 * k + 2 * half) * LANES
            results[start : start + 2 * LANES, :] = total

    for piece in range(4):
        swapped = block_swap(
            [
                results[pl.ds((q // 2) * LANES + q % 2 + 32 * piece, 16, stride=2), :]
                for q in range(N)
            ]
        )
        for a in range(N):
            start = a * N + 4 * piece
            x_out[start : start + 4] = swapped[a].reshape(4, 4, LANES).astype(BF16)
    me = row * N + col

    def tile_copy(other_row, other_col):
        return pltpu.make_async_remote_copy(
            src_ref=x_out.at[other_row * N + other_col], dst_ref=x_in.at[me],
            send_sem=tile_sems.at[0], recv_sem=tile_sems.at[1],
            device_id=(other_row, other_col), device_id_type=MESH,
        )

    for offset in COL_OFFSETS:
        other_col = col_at(col, offset)

        def one(i, carry, other_col=other_col):
            quarter = i // 4
            dx = jnp.where(quarter == 0, 2, jnp.where(quarter == 3, 0, 2 * quarter - 1))
            other_row = (
                ((row // 4 + dx) % 4) * 4
                + ((row // 2 + 1 - (i // 2) % 2) % 2) * 2
                + (row + 1 - i % 2) % 2
            )
            tile_copy(other_row, other_col).start()
            return carry

        lax.fori_loop(0, N - (1 if offset == (0, 0) else 0), one, 0)
    x_in[pl.ds(me, 1)] = x_out[pl.ds(me, 1)]

    place = lax.broadcasted_iota(jnp.int32, (K, 1), 0)
    member, device = place // (N * N), place % (N * N)
    perm[...] = one_hot(
        device // N + N * (2 * (device % N) + member) == momentum_map[...]
    )
    part, early, late = (place // CELLS) % 4, (place // TILE) % TILE, place % TILE
    lane = (late // 2) * LANES + ((member * 4 + part) * 2 + late % 2) * TILE + early
    select[...] = one_hot(lane == lax.broadcasted_iota(jnp.int32, (1, K), 1))
    everyone = pl.ds(0, N * N - 1)
    pltpu.make_async_copy(x_in.at[everyone], x_in.at[everyone], tile_sems.at[1]).wait()
    for d in range(N * N):
        spread[4 * d : 4 * d + 4, :] = x_in[d].astype(F32)
    rows = jnp.concatenate(
        [spread[pl.ds(i, N * N, stride=4), :] for i in range(4)], axis=1
    ).astype(BF16)
    cells = mm(select[...], rows, NT).astype(BF16)
    cells = jnp.concatenate([cells[: K // 2], cells[K // 2 :]], axis=1)
    final = mm(cells, perm[...]).astype(BF16)
    for half, out in enumerate((out_lesser, out_greater)):
        out[...] = (
            final[half * 2 * CELLS : (half + 1) * 2 * CELLS]
            .astype(F32)
            .reshape(2, TILE, TILE, K)
            .astype(BF16)
        )
    pltpu.make_async_copy(x_out.at[everyone], x_out.at[everyone], tile_sems.at[0]).wait()

    def passed_on(step, carry):
        other = lax.rem(row + step, N)

        @pl.when(other != col)
        def _():
            col_copy(site_in, mirror_in, MIRROR, other, col, plain).wait_send()

        return carry

    lax.fori_loop(0, N, passed_on, 0)
    rows_left(site_out, site_in, SITE)
    rows_left(ga_out, ga_in, GREEN_A)
    cols_left(gb_out, gb_in, GREEN_B, to_window)
    rows_left(y_out, y_in, INNER)
    cols_left(s_out, s_in, SIGMA, plain)


def sites_of(block):
    run = 32 * np.arange(16)
    if block == 0:
        return np.concatenate([run, 16 + run])
    return np.concatenate([block + run, (-block - run) % K])


def split(matrix):
    high = matrix.astype(jnp.bfloat16)
    low = (matrix - high.astype(np.float64)).astype(jnp.bfloat16)
    return np.concatenate([high, low], axis=-1)


def inverse_block(angle):
    cos, sin = np.cos(angle), np.sin(angle)
    return np.stack([np.stack([cos, sin], -1), np.stack([-sin, cos], -1)], -2)


def constants():
    order = (np.arange(K) // BLOCK) + N * (np.arange(K) % BLOCK)
    sites = np.concatenate([sites_of(block) for block in range(N)])
    phases = (sites[:, None] * order[None, :] % K).astype(np.float32) * np.float32(
        2.0 * math.pi / K
    )
    table = np.concatenate([np.cos(phases), np.sin(phases)], axis=1).astype(jnp.bfloat16)
    inner = np.zeros((N, N, 2, 2, 2, 2, 2, 2, 16))
    for block in range(N):
        near = sites_of(block).reshape(2, 16)
        angle = 2.0 * math.pi / K * (np.arange(N)[:, None, None] * near[None] % K)
        turn = inverse_block(angle)
        for half in range(2):
            for run in range(2):
                inner[block, :, half, :, run, half, :, run, :] = turn[:, run].transpose(0, 2, 3, 1)
    residues = np.array([[0, 16]] + [[b, 32 - b] for b in range(1, N)])
    angle = 2.0 * math.pi / 32 * (np.arange(32)[:, None, None] * residues[None] % 32)
    turn = inverse_block(angle)
    outer = np.zeros((32, 2, 2, N, 2, 2, 2))
    for half in range(2):
        outer[:, half, :, :, half] = turn.transpose(0, 3, 1, 4, 2)
    return table, split(inner.reshape(N, LANES, LANES)), split(outer.reshape(LANES, LANES))


def body(green_lesser, green_greater, lattice_map, time_offset):
    hbm = pl.BlockSpec(memory_space=pltpu.MemorySpace.HBM)
    vmem = pl.BlockSpec(memory_space=pltpu.MemorySpace.VMEM)
    tile = jax.ShapeDtypeStruct((2, TILE, TILE, K), BF16)
    by_row = pltpu.VMEM((N, 2, BLOCK, LANES), BF16)
    by_col = pltpu.VMEM((N, 2, 4, TILE, LANES), BF16)
    wide = pltpu.VMEM((N, TILE, WIDE), BF16)
    window = pltpu.VMEM((2, 4, N, TILE, LANES), BF16)
    halves = pltpu.VMEM((2, 2 * BLOCK, WIDE), BF16)
    return pl.pallas_call(
        kernel,
        out_shape=(tile, tile),
        in_specs=[pl.BlockSpec(memory_space=pltpu.MemorySpace.SMEM)] + [hbm] * 6,
        out_specs=(vmem, vmem),
        scratch_shapes=[
            pltpu.VMEM((1, K), jnp.int32),
            pltpu.VMEM((2, 2, TILE, TILE, K), BF16),
            pltpu.VMEM((K, 2 * K), BF16),
            pltpu.VMEM((LANES, 2 * LANES), BF16),
            pltpu.VMEM((LANES, 2 * LANES), BF16),
            pltpu.VMEM((K, K), BF16),
            pltpu.VMEM((2 * K, LANES), F32),
            halves, halves,
            pltpu.VMEM((LANES, WIDE), BF16),
            by_row, by_row, by_row,
            wide, wide, wide, wide,
            by_row, by_row, by_col, window,
            pltpu.VMEM((2, 2, 2 * LANES, 4 * LANES), BF16),
            pltpu.VMEM((2 * K, LANES), F32),
            pltpu.VMEM((K, K), BF16),
            pltpu.VMEM((N * N, 4, LANES), BF16),
            pltpu.VMEM((N * N, 4, LANES), BF16),
            pltpu.SemaphoreType.DMA((6,)),
            pltpu.SemaphoreType.DMA((6, N)),
            pltpu.SemaphoreType.DMA((6, N)),
            pltpu.SemaphoreType.DMA((2,)),
        ],
        compiler_params=pltpu.CompilerParams(
            collective_id=0, has_side_effects=True, vmem_limit_bytes=32 * 1024 * 1024
        ),
    )(
        time_offset,
        *(
            pltpu.with_memory_space_constraint(value, pltpu.MemorySpace.HBM)
            for value in (
                lattice_map.reshape(1, K), green_lesser, green_greater,
                *(jnp.asarray(value) for value in constants()),
            )
        ),
    )


def solution(mesh):
    in_specs = (P(None, "trow", "tcol", None), P(None, "trow", "tcol", None), P(), P())
    out_specs = (P(None, "trow", "tcol", None), P(None, "trow", "tcol", None))
    return jax.shard_map(body, mesh=mesh, in_specs=in_specs, out_specs=out_specs, check_vma=False)
```

```python
import math

import jax
import jax.numpy as jnp
import numpy as np
from jax import lax
from jax.experimental import pallas as pl
from jax.experimental.pallas import tpu as pltpu
from jax.sharding import PartitionSpec as P

PERIOD = 64
STEP_SIZE = 0.01
DRIVE_DEPTH = 0.5
MESH = pl.DeviceIdType.MESH
F32 = jnp.float32
BF16 = jnp.bfloat16

N = 16
TILE = 8
K = 512
BLOCK = K // N
LANES = N * TILE
WIDE = TILE * LANES
CELLS = TILE * TILE
NORM = 1.0 / math.sqrt(K)

NT = (((1,), (1,)), ((), ()))
NN = (((1,), (0,)), ((), ()))

SITE, MIRROR, GREEN_A, GREEN_B, INNER, SIGMA = 0, 1, 2, 3, (4, 5), (6, 7)

ROW_OFFSETS = sorted(
    ((x, y, c) for x in (2, 1, -1, 0) for y in (1, 0) for c in (0, 1)),
    key=lambda o: -(abs(o[0]) + o[1] + 0.2 * o[2]),
)[:-1]
COL_OFFSETS = sorted(
    ((y, z) for z in (4, 3, -3, 2, -2, 1, -1, 0) for y in (1, 0)),
    key=lambda o: -(abs(o[1]) + 2 * o[0]),
)


def row_at(row, offset, sign=1):
    x, y, c = row // 4, (row // 2) % 2, row % 2
    dx, dy, dc = offset
    return ((x + sign * dx + 4) % 4) * 4 + ((y + dy) % 2) * 2 + (c + dc) % 2


def col_at(col, offset, sign=1):
    y, z = col // 8, col % 8
    dy, dz = offset
    return ((y + dy) % 2) * 8 + (z + sign * dz + 8) % 8


def mm(left, right, dims=NN):
    return lax.dot_general(left, right, dims, preferred_element_type=F32)


def block_swap(parts):
    parts = list(parts)
    lane = lax.broadcasted_iota(jnp.int32, parts[0].shape, 1)
    bit = 1
    while bit < N:
        shift = bit * TILE
        low = (lane // shift) % 2 == 0
        for i in range(N):
            if i & bit:
                continue
            first, second = parts[i], parts[i | bit]
            parts[i] = jnp.where(low, first, pltpu.roll(second, shift, 1))
            parts[i | bit] = jnp.where(low, pltpu.roll(first, LANES - shift, 1), second)
        bit *= 2
    return parts


def one_hot(hit):
    return jnp.where(hit, 1.0, 0.0).astype(BF16)


def kernel(
    offset_ref, map_hbm, lesser_hbm, greater_hbm, table_hbm, inner_hbm, outer_hbm,
    out_lesser, out_greater,
    momentum_map, green, table, inner, outer, perm, spread, own, mirror,
    site_out, site_in, mirror_in, y_out, y_in, s_out, s_in,
    ga_out, ga_in, gb_out, gb_in, lefts, results, select, x_out, x_in,
    load_sems, send_sems, recv_sems, tile_sems,
):
    row = lax.axis_index("trow")
    col = lax.axis_index("tcol")
    barrier = pltpu.get_barrier_semaphore()

    loads = [
        pltpu.make_async_copy(source, target, load_sems.at[i])
        for i, (source, target) in enumerate(
            (
                (map_hbm, momentum_map),
                (lesser_hbm, green.at[0]),
                (greater_hbm, green.at[1]),
                (table_hbm, table),
                (outer_hbm, outer),
                (inner_hbm.at[row], inner),
            )
        )
    ]
    for load in loads:
        load.start()
    for offset in COL_OFFSETS[:-1]:
        pl.semaphore_signal(
            barrier, inc=1, device_id=(row, col_at(col, offset)), device_id_type=MESH
        )
    for offset in ROW_OFFSETS:
        pl.semaphore_signal(
            barrier, inc=1, device_id=(row_at(row, offset), col), device_id_type=MESH
        )

    def plain(ref, i):
        return ref.at[i]

    def in_window(ref, i):
        return ref.at[:, :, i]

    def lane_half(part):
        return lambda ref, i: ref.at[i, :, pl.ds(part * (WIDE // 2), WIDE // 2)]

    to_window = (plain, in_window)
    plain = (plain, plain)
    lane_halves = [(lane_half(part), lane_half(part)) for part in range(2)]

    def row_copy(source, target, phase, other, slot, form=plain):
        return pltpu.make_async_remote_copy(
            src_ref=form[0](source, other), dst_ref=form[1](target, slot),
            send_sem=send_sems.at[phase, other], recv_sem=recv_sems.at[phase, slot],
            device_id=(other, col), device_id_type=MESH,
        )

    def along_rows(source, target, phase, form=plain):
        for offset in ROW_OFFSETS:
            row_copy(source, target, phase, row_at(row, offset), row, form).start()

    def rows_arrived(source, target, phase, form=plain):
        for offset in ROW_OFFSETS:
            other = row_at(row, offset, -1)
            row_copy(source, target, phase, other, other, form).wait_recv()

    def rows_left(source, target, phase, form=plain):
        for offset in ROW_OFFSETS:
            row_copy(source, target, phase, row_at(row, offset), row, form).wait_send()

    def col_copy(source, target, phase, other, slot, form):
        return pltpu.make_async_remote_copy(
            src_ref=form[0](source, other), dst_ref=form[1](target, slot),
            send_sem=send_sems.at[phase, other], recv_sem=recv_sems.at[phase, slot],
            device_id=(row, other), device_id_type=MESH,
        )

    def along_cols(source, target, phase, form):
        for offset in COL_OFFSETS[:-1]:
            col_copy(source, target, phase, col_at(col, offset), col, form).start()

    def cols_arrived(source, target, phase, form):
        for offset in COL_OFFSETS[:-1]:
            other = col_at(col, offset, -1)
            col_copy(source, target, phase, other, other, form).wait_recv()

    def cols_left(source, target, phase, form):
        for offset in COL_OFFSETS[:-1]:
            col_copy(source, target, phase, col_at(col, offset), col, form).wait_send()

    place = lax.broadcasted_iota(jnp.int32, (K, 1), 0)
    loads[0].wait()
    perm[...] = one_hot((place // BLOCK) + N * (place % BLOCK) == momentum_map[...])
    r = lax.broadcasted_iota(jnp.int32, (LANES, LANES), 0)
    c = lax.broadcasted_iota(jnp.int32, (LANES, LANES), 1)
    swap = one_hot(
        (r // CELLS == c // CELLS)
        & ((r // TILE) % TILE == c % TILE)
        & (r % TILE == (c // TILE) % TILE)
    )

    loads[1].wait()
    loads[2].wait()
    pairs = []
    natural = jnp.concatenate(
        [green[half].astype(F32).reshape(2 * CELLS, K) for half in range(2)], axis=0
    ).astype(BF16)
    ordered = mm(natural, perm[...], NT)
    for half in range(2):
        g_re = ordered[2 * half * CELLS : (2 * half + 1) * CELLS]
        g_im = ordered[(2 * half + 1) * CELLS : (2 * half + 2) * CELLS]
        pairs.append(jnp.concatenate([g_re, -g_im], axis=1))
        pairs.append(jnp.concatenate([g_im, g_re], axis=1))
    pairs = jnp.concatenate(pairs, axis=0).astype(BF16)
    loads[3].wait()
    sites = mm(table[...], pairs, NT) * NORM
    for half in range(2):
        site_out[:, half] = (
            sites[:, half * LANES : (half + 1) * LANES].reshape(N, BLOCK, LANES).astype(BF16)
        )

    pl.semaphore_wait(barrier, 2 * (N - 1))
    along_rows(site_out, site_in, SITE)
    site_in[pl.ds(row, 1)] = site_out[pl.ds(row, 1)]
    spectral = mm(perm[...], natural, NT)
    for half in range(2):
        ga_out[:, half] = (
            spectral[:, half * LANES : (half + 1) * LANES].reshape(N, BLOCK, LANES).astype(BF16)
        )

    def pass_on(other):
        @pl.when(other != col)
        def _():
            col_copy(site_in, mirror_in, MIRROR, other, col, plain).start()

        @pl.when(other == col)
        def _():
            mirror_in[pl.ds(col, 1)] = site_in[pl.ds(col, 1)]

    pass_on(row)

    for offset in ROW_OFFSETS:
        other = row_at(row, offset, -1)
        row_copy(site_out, site_in, SITE, other, other).wait_recv()
        pass_on(other)
    along_rows(ga_out, ga_in, GREEN_A)
    ga_in[pl.ds(row, 1)] = ga_out[pl.ds(row, 1)]

    def pieces(ref, half, base):
        return [
            ref[pl.ds(i * 2 * BLOCK + half * BLOCK + base, 16), :] for i in range(N)
        ]

    def to_rows(target, half, base, swapped):
        for q in range(N):
            at, lane = (q // TILE) * BLOCK + base, (q % TILE) * LANES
            target[half, at : at + 16, lane : lane + LANES] = swapped[q].astype(BF16)

    spread[...] = mm(site_in[...].reshape(2 * K, LANES), swap)
    for half in range(2):
        for base in (0, 16):
            to_rows(own, half, base, block_swap(pieces(spread, half, base)))

    rows_arrived(ga_out, ga_in, GREEN_A)
    results[...] = mm(ga_in[...].reshape(2 * K, LANES), swap)
    for half in range(2):
        for base in (0, 16):
            swapped = block_swap(pieces(results, half, base))
            for q in range(N):
                start = (half * N + q) * BLOCK + base
                spread[start : start + 16, :] = swapped[q]
    for m in range(BLOCK):
        picked = spread[pl.ds(m, BLOCK, stride=BLOCK), :]
        gb_out[m // 2, m % 2] = picked.reshape(4, TILE, LANES).astype(BF16)
    gb_in[:, :, pl.ds(col, 1)] = gb_out[pl.ds(col, 1)].reshape(2, 4, 1, TILE, LANES)

    steps = lax.broadcasted_iota(jnp.int32, (TILE, LANES), 1)
    late = lax.broadcasted_iota(jnp.int32, (TILE, LANES), 0) + col * TILE

    def drive(at):
        phase = ((offset_ref[0] + at) % PERIOD).astype(F32) * (2.0 * math.pi / PERIOD)
        return 1.0 + DRIVE_DEPTH * jnp.cos(phase)

    product = drive(late) * drive(steps)
    coupling = jnp.concatenate([product[i : i + 1] for i in range(TILE)], axis=1)
    fr = lax.broadcasted_iota(jnp.int32, (2 * BLOCK, 2 * BLOCK), 0)
    fc = lax.broadcasted_iota(jnp.int32, (2 * BLOCK, 2 * BLOCK), 1)
    first_run = (fc // 16) % 2 == 0
    inside = fc + jnp.where(first_run, 16, -16)
    edge = (fc // 16) * 16 + jnp.where(first_run, (16 - fc % 16) % 16, 15 - fc % 16)
    flip = one_hot(fr == inside + jnp.where(row == 0, 1, 0) * (edge - inside))

    along_cols(gb_out, gb_in, GREEN_B, to_window)
    cols_arrived(site_in, mirror_in, MIRROR, plain)
    for half in range(2):
        for base in (0, 16):
            arrived = [mirror_in[b, half, base : base + 16, :].astype(F32) for b in range(N)]
            to_rows(mirror, half, base, block_swap(arrived))
    loads[5].wait()
    for part in range(2):
        lanes = slice(part * (WIDE // 2), (part + 1) * (WIDE // 2))
        weight = coupling[:, lanes]
        selves = []
        for half in range(2):
            first_re = own[half, :BLOCK, lanes].astype(F32)
            first_im = own[half, BLOCK:, lanes].astype(F32)
            other = mm(flip, mirror[1 - half, :, lanes])
            other_re, other_im = other[:BLOCK], other[BLOCK:]
            square_re = first_re * first_re - first_im * first_im
            square_im = 2.0 * first_re * first_im
            selves.append(weight * (square_re * other_re - square_im * other_im))
            selves.append(weight * (square_re * other_im + square_im * other_re))
        selves = jnp.concatenate(selves, axis=0).astype(BF16)
        terms = mm(inner[...], jnp.concatenate([selves, selves], axis=0))
        y_out[:, :, lanes] = terms.reshape(N, TILE, WIDE // 2).astype(BF16)
        along_rows(y_out, y_in, INNER[part], lane_halves[part])
    y_in[pl.ds(row, 1)] = y_out[pl.ds(row, 1)]

    down = lax.broadcasted_iota(jnp.int32, (LANES, LANES), 0)
    across = lax.broadcasted_iota(jnp.int32, (LANES, LANES), 1)
    cols_arrived(gb_out, gb_in, GREEN_B, to_window)
    for k in range(2):
        g = [gb_in[k, i].astype(F32).reshape(LANES, LANES) for i in range(4)]
        advanced = [jnp.where(across <= down, g[i] - g[2 + i], 0.0) for i in range(2)]
        for half in range(2):
            g_re, g_im = g[2 * half], g[2 * half + 1]
            for i, blocks in enumerate(
                ([g_re, -g_im, advanced[0], -advanced[1]], [g_im, g_re, advanced[1], advanced[0]])
            ):
                lefts[k, half, i * LANES : (i + 1) * LANES, :] = jnp.concatenate(
                    blocks, axis=1
                ).astype(BF16)

    loads[4].wait()
    for part in range(2):
        lanes = slice(part * (WIDE // 2), (part + 1) * (WIDE // 2))
        rows_arrived(y_out, y_in, INNER[part], lane_halves[part])
        arrived = y_in[:, :, lanes].astype(F32).reshape(LANES, WIDE // 2).astype(BF16)
        sigma = mm(outer[...], jnp.concatenate([arrived, arrived], axis=0)) * NORM
        s_out[:, :, lanes] = sigma.reshape(N, TILE, WIDE // 2).astype(BF16)
        along_cols(s_out, s_in, SIGMA[part], lane_halves[part])
    s_in[pl.ds(col, 1)] = s_out[pl.ds(col, 1)]
    for part in range(2):
        cols_arrived(s_out, s_in, SIGMA[part], lane_halves[part])
        for b in range(N):
            for t in range(part * TILE // 2, (part + 1) * TILE // 2):
                start = (b * TILE + t) * TILE
                spread[start : start + TILE, :] = s_in[
                    b, :, t * LANES : (t + 1) * LANES
                ].astype(F32)
    for k in range(2):
        s = [spread[pl.ds(4 * k + i, LANES, stride=TILE), :] for i in range(4)]
        retarded = [jnp.where(down <= across, s[2 + i] - s[i], 0.0) for i in range(2)]
        for half in range(2):
            right = jnp.concatenate(
                retarded + [s[2 * half], s[2 * half + 1]], axis=0
            ).astype(BF16)
            total = mm(lefts[k, half], right) * STEP_SIZE
            start = (4 * k + 2 * half) * LANES
            results[start : start + 2 * LANES, :] = total

    for piece in range(4):
        swapped = block_swap(
            [
                results[pl.ds((q // 2) * LANES + q % 2 + 32 * piece, 16, stride=2), :]
                for q in range(N)
            ]
        )
        for a in range(N):
            start = a * N + 4 * piece
            x_out[start : start + 4] = swapped[a].reshape(4, 4, LANES).astype(BF16)
    me = row * N + col

    def tile_copy(other_row, other_col):
        return pltpu.make_async_remote_copy(
            src_ref=x_out.at[other_row * N + other_col], dst_ref=x_in.at[me],
            send_sem=tile_sems.at[0], recv_sem=tile_sems.at[1],
            device_id=(other_row, other_col), device_id_type=MESH,
        )

    for offset in COL_OFFSETS:
        other_col = col_at(col, offset)

        def one(i, carry, other_col=other_col):
            quarter = i // 4
            dx = jnp.where(quarter == 0, 2, jnp.where(quarter == 3, 0, 2 * quarter - 1))
            other_row = (
                ((row // 4 + dx) % 4) * 4
                + ((row // 2 + 1 - (i // 2) % 2) % 2) * 2
                + (row + 1 - i % 2) % 2
            )
            tile_copy(other_row, other_col).start()
            return carry

        lax.fori_loop(0, N - (1 if offset == (0, 0) else 0), one, 0)
    x_in[pl.ds(me, 1)] = x_out[pl.ds(me, 1)]

    place = lax.broadcasted_iota(jnp.int32, (K, 1), 0)
    member, device = place // (N * N), place % (N * N)
    perm[...] = one_hot(
        device // N + N * (2 * (device % N) + member) == momentum_map[...]
    )
    part, early, late = (place // CELLS) % 4, (place // TILE) % TILE, place % TILE
    lane = (late // 2) * LANES + ((member * 4 + part) * 2 + late % 2) * TILE + early
    select[...] = one_hot(lane == lax.broadcasted_iota(jnp.int32, (1, K), 1))
    everyone = pl.ds(0, N * N - 1)
    pltpu.make_async_copy(x_in.at[everyone], x_in.at[everyone], tile_sems.at[1]).wait()
    for d in range(N * N):
        spread[4 * d : 4 * d + 4, :] = x_in[d].astype(F32)
    rows = jnp.concatenate(
        [spread[pl.ds(i, N * N, stride=4), :] for i in range(4)], axis=1
    ).astype(BF16)
    cells = mm(select[...], rows, NT).astype(BF16)
    cells = jnp.concatenate([cells[: K // 2], cells[K // 2 :]], axis=1)
    final = mm(cells, perm[...]).astype(BF16)
    for half, out in enumerate((out_lesser, out_greater)):
        out[...] = (
            final[half * 2 * CELLS : (half + 1) * 2 * CELLS]
            .astype(F32)
            .reshape(2, TILE, TILE, K)
            .astype(BF16)
        )
    pltpu.make_async_copy(x_out.at[everyone], x_out.at[everyone], tile_sems.at[0]).wait()

    def passed_on(step, carry):
        other = lax.rem(row + step, N)

        @pl.when(other != col)
        def _():
            col_copy(site_in, mirror_in, MIRROR, other, col, plain).wait_send()

        return carry

    lax.fori_loop(0, N, passed_on, 0)
    rows_left(site_out, site_in, SITE)
    rows_left(ga_out, ga_in, GREEN_A)
    cols_left(gb_out, gb_in, GREEN_B, to_window)
    for part in range(2):
        rows_left(y_out, y_in, INNER[part], lane_halves[part])
        cols_left(s_out, s_in, SIGMA[part], lane_halves[part])


def sites_of(block):
    run = 32 * np.arange(16)
    if block == 0:
        return np.concatenate([run, 16 + run])
    return np.concatenate([block + run, (-block - run) % K])


def split(matrix):
    high = matrix.astype(jnp.bfloat16)
    low = (matrix - high.astype(np.float64)).astype(jnp.bfloat16)
    return np.concatenate([high, low], axis=-1)


def inverse_block(angle):
    cos, sin = np.cos(angle), np.sin(angle)
    return np.stack([np.stack([cos, sin], -1), np.stack([-sin, cos], -1)], -2)


def constants():
    order = (np.arange(K) // BLOCK) + N * (np.arange(K) % BLOCK)
    sites = np.concatenate([sites_of(block) for block in range(N)])
    phases = (sites[:, None] * order[None, :] % K).astype(np.float32) * np.float32(
        2.0 * math.pi / K
    )
    table = np.concatenate([np.cos(phases), np.sin(phases)], axis=1).astype(jnp.bfloat16)
    inner = np.zeros((N, N, 2, 2, 2, 2, 2, 2, 16))
    for block in range(N):
        near = sites_of(block).reshape(2, 16)
        angle = 2.0 * math.pi / K * (np.arange(N)[:, None, None] * near[None] % K)
        turn = inverse_block(angle)
        for half in range(2):
            for run in range(2):
                inner[block, :, half, :, run, half, :, run, :] = turn[:, run].transpose(0, 2, 3, 1)
    residues = np.array([[0, 16]] + [[b, 32 - b] for b in range(1, N)])
    angle = 2.0 * math.pi / 32 * (np.arange(32)[:, None, None] * residues[None] % 32)
    turn = inverse_block(angle)
    outer = np.zeros((32, 2, 2, N, 2, 2, 2))
    for half in range(2):
        outer[:, half, :, :, half] = turn.transpose(0, 3, 1, 4, 2)
    return table, split(inner.reshape(N, LANES, LANES)), split(outer.reshape(LANES, LANES))


def body(green_lesser, green_greater, lattice_map, time_offset):
    hbm = pl.BlockSpec(memory_space=pltpu.MemorySpace.HBM)
    vmem = pl.BlockSpec(memory_space=pltpu.MemorySpace.VMEM)
    tile = jax.ShapeDtypeStruct((2, TILE, TILE, K), BF16)
    by_row = pltpu.VMEM((N, 2, BLOCK, LANES), BF16)
    by_col = pltpu.VMEM((N, 2, 4, TILE, LANES), BF16)
    wide = pltpu.VMEM((N, TILE, WIDE), BF16)
    window = pltpu.VMEM((2, 4, N, TILE, LANES), BF16)
    halves = pltpu.VMEM((2, 2 * BLOCK, WIDE), BF16)
    return pl.pallas_call(
        kernel,
        out_shape=(tile, tile),
        in_specs=[pl.BlockSpec(memory_space=pltpu.MemorySpace.SMEM)] + [hbm] * 6,
        out_specs=(vmem, vmem),
        scratch_shapes=[
            pltpu.VMEM((1, K), jnp.int32),
            pltpu.VMEM((2, 2, TILE, TILE, K), BF16),
            pltpu.VMEM((K, 2 * K), BF16),
            pltpu.VMEM((LANES, 2 * LANES), BF16),
            pltpu.VMEM((LANES, 2 * LANES), BF16),
            pltpu.VMEM((K, K), BF16),
            pltpu.VMEM((2 * K, LANES), F32),
            halves, halves,
            by_row, by_row, by_row,
            wide, wide, wide, wide,
            by_row, by_row, by_col, window,
            pltpu.VMEM((2, 2, 2 * LANES, 4 * LANES), BF16),
            pltpu.VMEM((2 * K, LANES), F32),
            pltpu.VMEM((K, K), BF16),
            pltpu.VMEM((N * N, 4, LANES), BF16),
            pltpu.VMEM((N * N, 4, LANES), BF16),
            pltpu.SemaphoreType.DMA((6,)),
            pltpu.SemaphoreType.DMA((8, N)),
            pltpu.SemaphoreType.DMA((8, N)),
            pltpu.SemaphoreType.DMA((2,)),
        ],
        compiler_params=pltpu.CompilerParams(
            collective_id=0, has_side_effects=True, vmem_limit_bytes=32 * 1024 * 1024
        ),
    )(
        time_offset,
        *(
            pltpu.with_memory_space_constraint(value, pltpu.MemorySpace.HBM)
            for value in (
                lattice_map.reshape(1, K), green_lesser, green_greater,
                *(jnp.asarray(value) for value in constants()),
            )
        ),
    )


def solution(mesh):
    in_specs = (P(None, "trow", "tcol", None), P(None, "trow", "tcol", None), P(), P())
    out_specs = (P(None, "trow", "tcol", None), P(None, "trow", "tcol", None))
    return jax.shard_map(body, mesh=mesh, in_specs=in_specs, out_specs=out_specs, check_vma=False)
```

```python
import math

import jax
import jax.numpy as jnp
import numpy as np
from jax import lax
from jax.experimental import pallas as pl
from jax.experimental.pallas import tpu as pltpu
from jax.sharding import PartitionSpec as P

PERIOD = 64
STEP_SIZE = 0.01
DRIVE_DEPTH = 0.5
MESH = pl.DeviceIdType.MESH
F32 = jnp.float32
BF16 = jnp.bfloat16

N = 16
TILE = 8
K = 512
BLOCK = K // N
LANES = N * TILE
WIDE = TILE * LANES
CELLS = TILE * TILE
NORM = 1.0 / math.sqrt(K)

NT = (((1,), (1,)), ((), ()))
NN = (((1,), (0,)), ((), ()))

SITE, MIRROR, INNER, SIGMA, GREEN_A, GREEN_B = range(6)

ROW_OFFSETS = sorted(
    ((x, y, c) for x in (2, 1, -1, 0) for y in (1, 0) for c in (0, 1)),
    key=lambda o: -(abs(o[0]) + o[1] + 0.2 * o[2]),
)[:-1]
COL_OFFSETS = sorted(
    ((y, z) for z in (4, 3, -3, 2, -2, 1, -1, 0) for y in (1, 0)),
    key=lambda o: -(abs(o[1]) + 2 * o[0]),
)


def row_at(row, offset, sign=1):
    x, y, c = row // 4, (row // 2) % 2, row % 2
    dx, dy, dc = offset
    return ((x + sign * dx + 4) % 4) * 4 + ((y + dy) % 2) * 2 + (c + dc) % 2


def col_at(col, offset, sign=1):
    y, z = col // 8, col % 8
    dy, dz = offset
    return ((y + dy) % 2) * 8 + (z + sign * dz + 8) % 8


def mm(left, right, dims=NN):
    return lax.dot_general(left, right, dims, preferred_element_type=F32)


def block_swap(parts):
    parts = list(parts)
    lane = lax.broadcasted_iota(jnp.int32, parts[0].shape, 1)
    bit = 1
    while bit < N:
        shift = bit * TILE
        low = (lane // shift) % 2 == 0
        for i in range(N):
            if i & bit:
                continue
            first, second = parts[i], parts[i | bit]
            parts[i] = jnp.where(low, first, pltpu.roll(second, shift, 1))
            parts[i | bit] = jnp.where(low, pltpu.roll(first, LANES - shift, 1), second)
        bit *= 2
    return parts


def one_hot(hit):
    return jnp.where(hit, 1.0, 0.0).astype(BF16)


def kernel(
    offset_ref, map_hbm, lesser_hbm, greater_hbm, table_hbm, inner_hbm, outer_hbm,
    out_lesser, out_greater,
    momentum_map, green, table, inner, outer, perm, spread, own, mirror, selves,
    site_out, site_in, mirror_in, y_out, y_in, s_out, s_in,
    ga_out, ga_in, gb_out, gb_in, lefts, results, select, x_out, x_in,
    load_sems, send_sems, recv_sems, tile_sems,
):
    row = lax.axis_index("trow")
    col = lax.axis_index("tcol")
    barrier = pltpu.get_barrier_semaphore()

    loads = [
        pltpu.make_async_copy(source, target, load_sems.at[i])
        for i, (source, target) in enumerate(
            (
                (map_hbm, momentum_map),
                (lesser_hbm, green.at[0]),
                (greater_hbm, green.at[1]),
                (table_hbm, table),
                (outer_hbm, outer),
                (inner_hbm.at[row], inner),
            )
        )
    ]
    for load in loads:
        load.start()
    for offset in COL_OFFSETS[:-1]:
        pl.semaphore_signal(
            barrier, inc=1, device_id=(row, col_at(col, offset)), device_id_type=MESH
        )
    for offset in ROW_OFFSETS:
        pl.semaphore_signal(
            barrier, inc=1, device_id=(row_at(row, offset), col), device_id_type=MESH
        )

    def row_copy(source, target, phase, other, slot):
        return pltpu.make_async_remote_copy(
            src_ref=source.at[other], dst_ref=target.at[slot],
            send_sem=send_sems.at[phase, other], recv_sem=recv_sems.at[phase, slot],
            device_id=(other, col), device_id_type=MESH,
        )

    def along_rows(source, target, phase):
        for offset in ROW_OFFSETS:
            row_copy(source, target, phase, row_at(row, offset), row).start()
        target[pl.ds(row, 1)] = source[pl.ds(row, 1)]

    def rows_arrived(source, target, phase):
        for offset in ROW_OFFSETS:
            other = row_at(row, offset, -1)
            row_copy(source, target, phase, other, other).wait_recv()

    def rows_left(source, target, phase):
        for offset in ROW_OFFSETS:
            row_copy(source, target, phase, row_at(row, offset), row).wait_send()

    plain = (lambda ref, i: ref.at[i], lambda ref, i: ref.at[i])
    to_window = (lambda ref, i: ref.at[i], lambda ref, i: ref.at[:, :, i])

    def col_copy(source, target, phase, other, slot, form):
        return pltpu.make_async_remote_copy(
            src_ref=form[0](source, other), dst_ref=form[1](target, slot),
            send_sem=send_sems.at[phase, other], recv_sem=recv_sems.at[phase, slot],
            device_id=(row, other), device_id_type=MESH,
        )

    def along_cols(source, target, phase, form):
        for offset in COL_OFFSETS[:-1]:
            col_copy(source, target, phase, col_at(col, offset), col, form).start()

    def cols_arrived(source, target, phase, form):
        for offset in COL_OFFSETS[:-1]:
            other = col_at(col, offset, -1)
            col_copy(source, target, phase, other, other, form).wait_recv()

    def cols_left(source, target, phase, form):
        for offset in COL_OFFSETS[:-1]:
            col_copy(source, target, phase, col_at(col, offset), col, form).wait_send()

    place = lax.broadcasted_iota(jnp.int32, (K, 1), 0)
    loads[0].wait()
    perm[...] = one_hot((place // BLOCK) + N * (place % BLOCK) == momentum_map[...])
    r = lax.broadcasted_iota(jnp.int32, (LANES, LANES), 0)
    c = lax.broadcasted_iota(jnp.int32, (LANES, LANES), 1)
    swap = one_hot(
        (r // CELLS == c // CELLS)
        & ((r // TILE) % TILE == c % TILE)
        & (r % TILE == (c // TILE) % TILE)
    )

    loads[1].wait()
    loads[2].wait()
    turned = []
    pairs = []
    for half in range(2):
        natural = green[half].astype(F32).reshape(2 * CELLS, K).astype(BF16)
        turned.append(mm(swap, natural).astype(BF16))
    turned = jnp.concatenate(turned, axis=0)
    ordered = mm(turned, perm[...], NT)
    for half in range(2):
        g_re = ordered[2 * half * CELLS : (2 * half + 1) * CELLS]
        g_im = ordered[(2 * half + 1) * CELLS : (2 * half + 2) * CELLS]
        pairs.append(jnp.concatenate([g_re, -g_im], axis=1))
        pairs.append(jnp.concatenate([g_im, g_re], axis=1))
    pairs = jnp.concatenate(pairs, axis=0).astype(BF16)
    loads[3].wait()
    sites = mm(table[...], pairs, NT) * NORM
    for half in range(2):
        site_out[:, half] = (
            sites[:, half * LANES : (half + 1) * LANES].reshape(N, BLOCK, LANES).astype(BF16)
        )

    pl.semaphore_wait(barrier, 2 * (N - 1))
    along_rows(site_out, site_in, SITE)
    spectral = mm(perm[...], turned, NT)
    for half in range(2):
        ga_out[:, half] = (
            spectral[:, half * LANES : (half + 1) * LANES].reshape(N, BLOCK, LANES).astype(BF16)
        )

    def pass_on(other):
        @pl.when(other != col)
        def _():
            col_copy(site_in, mirror_in, MIRROR, other, col, plain).start()

        @pl.when(other == col)
        def _():
            mirror_in[pl.ds(col, 1)] = site_in[pl.ds(col, 1)]

    pass_on(row)

    for offset in ROW_OFFSETS:
        other = row_at(row, offset, -1)
        row_copy(site_out, site_in, SITE, other, other).wait_recv()
        pass_on(other)
        row_copy(ga_out, ga_in, GREEN_A, row_at(row, offset), row).start()
    ga_in[pl.ds(row, 1)] = ga_out[pl.ds(row, 1)]

    for half in range(2):
        for part in range(2):
            base = part * 16
            swapped = block_swap(
                [site_in[a, half, base : base + 16, :].astype(F32) for a in range(N)]
            )
            for q in range(N):
                at, lane = (q // TILE) * BLOCK + base, (q % TILE) * LANES
                own[half, at : at + 16, lane : lane + LANES] = swapped[q].astype(BF16)

    rows_arrived(ga_out, ga_in, GREEN_A)
    for half in range(2):
        for part in range(2):
            base = part * 16
            swapped = block_swap(
                [ga_in[a, half, base : base + 16, :].astype(F32) for a in range(N)]
            )
            for q in range(N):
                start = (half * N + q) * BLOCK + base
                spread[start : start + 16, :] = swapped[q]
    for m in range(BLOCK):
        picked = spread[pl.ds(m, BLOCK, stride=BLOCK), :]
        gb_out[m // 2, m % 2] = picked.reshape(4, TILE, LANES).astype(BF16)
    gb_in[:, :, pl.ds(col, 1)] = gb_out[pl.ds(col, 1)].reshape(2, 4, 1, TILE, LANES)

    steps = lax.broadcasted_iota(jnp.int32, (TILE, LANES), 1)
    late = lax.broadcasted_iota(jnp.int32, (TILE, LANES), 0) + col * TILE

    def drive(at):
        phase = ((offset_ref[0] + at) % PERIOD).astype(F32) * (2.0 * math.pi / PERIOD)
        return 1.0 + DRIVE_DEPTH * jnp.cos(phase)

    product = drive(late) * drive(steps)
    coupling = jnp.concatenate([product[i : i + 1] for i in range(TILE)], axis=1)
    fr = lax.broadcasted_iota(jnp.int32, (2 * BLOCK, 2 * BLOCK), 0)
    fc = lax.broadcasted_iota(jnp.int32, (2 * BLOCK, 2 * BLOCK), 1)
    first_run = (fc // 16) % 2 == 0
    inside = fc + jnp.where(first_run, 16, -16)
    edge = (fc // 16) * 16 + jnp.where(first_run, (16 - fc % 16) % 16, 15 - fc % 16)
    flip = one_hot(fr == inside + jnp.where(row == 0, 1, 0) * (edge - inside))

    along_cols(gb_out, gb_in, GREEN_B, to_window)
    cols_arrived(site_in, mirror_in, MIRROR, plain)
    spread[...] = mm(mirror_in[...].reshape(2 * K, LANES), swap)
    for half in range(2):
        for part in range(2):
            base = part * 16
            swapped = block_swap(
                [
                    spread[pl.ds(b * 2 * BLOCK + half * BLOCK + base, 16), :]
                    for b in range(N)
                ]
            )
            for q in range(N):
                at, lane = (q // TILE) * BLOCK + base, (q % TILE) * LANES
                mirror[half, at : at + 16, lane : lane + LANES] = swapped[q].astype(BF16)
    for half in range(2):
        first_re, first_im = own[half, :BLOCK].astype(F32), own[half, BLOCK:].astype(F32)
        other = mm(flip, mirror[1 - half])
        other_re, other_im = other[:BLOCK], other[BLOCK:]
        square_re = first_re * first_re - first_im * first_im
        square_im = 2.0 * first_re * first_im
        self_re = coupling * (square_re * other_re - square_im * other_im)
        self_im = coupling * (square_re * other_im + square_im * other_re)
        at = half * 2 * BLOCK
        selves[at : at + BLOCK] = self_re.astype(BF16)
        selves[at + BLOCK : at + 2 * BLOCK] = self_im.astype(BF16)
    doubled = jnp.concatenate([selves[...], selves[...]], axis=0)
    loads[5].wait()
    y_out[...] = mm(inner[...], doubled).reshape(N, TILE, WIDE).astype(BF16)
    along_rows(y_out, y_in, INNER)

    down = lax.broadcasted_iota(jnp.int32, (LANES, LANES), 0)
    across = lax.broadcasted_iota(jnp.int32, (LANES, LANES), 1)
    cols_arrived(gb_out, gb_in, GREEN_B, to_window)
    for k in range(2):
        g = [gb_in[k, i].astype(F32).reshape(LANES, LANES) for i in range(4)]
        advanced = [jnp.where(across <= down, g[i] - g[2 + i], 0.0) for i in range(2)]
        for half in range(2):
            g_re, g_im = g[2 * half], g[2 * half + 1]
            for i, blocks in enumerate(
                ([g_re, -g_im, advanced[0], -advanced[1]], [g_im, g_re, advanced[1], advanced[0]])
            ):
                lefts[k, half, i * LANES : (i + 1) * LANES, :] = jnp.concatenate(
                    blocks, axis=1
                ).astype(BF16)

    loads[4].wait()
    rows_arrived(y_out, y_in, INNER)
    arrived = y_in[...].astype(F32).reshape(LANES, WIDE).astype(BF16)
    sigma = mm(outer[...], jnp.concatenate([arrived, arrived], axis=0)) * NORM
    s_out[...] = sigma.reshape(N, TILE, WIDE).astype(BF16)
    along_cols(s_out, s_in, SIGMA, plain)
    s_in[pl.ds(col, 1)] = s_out[pl.ds(col, 1)]
    cols_arrived(s_out, s_in, SIGMA, plain)
    for b in range(N):
        for t in range(TILE):
            start = (b * TILE + t) * TILE
            spread[start : start + TILE, :] = s_in[b, :, t * LANES : (t + 1) * LANES].astype(F32)
    for k in range(2):
        s = [spread[pl.ds(4 * k + i, LANES, stride=TILE), :] for i in range(4)]
        retarded = [jnp.where(down <= across, s[2 + i] - s[i], 0.0) for i in range(2)]
        for half in range(2):
            right = jnp.concatenate(
                retarded + [s[2 * half], s[2 * half + 1]], axis=0
            ).astype(BF16)
            total = mm(lefts[k, half], right) * STEP_SIZE
            start = (4 * k + 2 * half) * LANES
            results[start : start + 2 * LANES, :] = total

    for piece in range(4):
        swapped = block_swap(
            [
                results[pl.ds((q // 2) * LANES + q % 2 + 32 * piece, 16, stride=2), :]
                for q in range(N)
            ]
        )
        for a in range(N):
            start = a * N + 4 * piece
            x_out[start : start + 4] = swapped[a].reshape(4, 4, LANES).astype(BF16)
    me = row * N + col

    def tile_copy(other_row, other_col):
        return pltpu.make_async_remote_copy(
            src_ref=x_out.at[other_row * N + other_col], dst_ref=x_in.at[me],
            send_sem=tile_sems.at[0], recv_sem=tile_sems.at[1],
            device_id=(other_row, other_col), device_id_type=MESH,
        )

    row_ids = [row_at(row, offset) for offset in ROW_OFFSETS] + [row]
    col_ids = [col_at(col, offset) for offset in COL_OFFSETS]
    row_far = [abs(o[0]) + o[1] + 0.2 * o[2] for o in ROW_OFFSETS] + [0.0]
    col_far = [abs(o[1]) + 2 * o[0] for o in COL_OFFSETS]
    order = sorted(
        ((i, j) for j in range(N) for i in range(N)), key=lambda p: -(row_far[p[0]] + col_far[p[1]])
    )[:-1]
    for i, j in order:
        tile_copy(row_ids[i], col_ids[j]).start()
    x_in[pl.ds(me, 1)] = x_out[pl.ds(me, 1)]

    place = lax.broadcasted_iota(jnp.int32, (K, 1), 0)
    member, device = place // (N * N), place % (N * N)
    perm[...] = one_hot(
        device // N + N * (2 * (device % N) + member) == momentum_map[...]
    )
    part, early, late = (place // CELLS) % 4, (place // TILE) % TILE, place % TILE
    lane = (late // 2) * LANES + ((member * 4 + part) * 2 + late % 2) * TILE + early
    select[...] = one_hot(lane == lax.broadcasted_iota(jnp.int32, (1, K), 1))
    everyone = pl.ds(0, N * N - 1)
    pltpu.make_async_copy(x_in.at[everyone], x_in.at[everyone], tile_sems.at[1]).wait()
    for d in range(N * N):
        spread[4 * d : 4 * d + 4, :] = x_in[d].astype(F32)
    rows = jnp.concatenate(
        [spread[pl.ds(i, N * N, stride=4), :] for i in range(4)], axis=1
    ).astype(BF16)
    cells = mm(select[...], rows, NT).astype(BF16)
    cells = jnp.concatenate([cells[: K // 2], cells[K // 2 :]], axis=1)
    final = mm(cells, perm[...]).astype(BF16)
    for half, out in enumerate((out_lesser, out_greater)):
        out[...] = (
            final[half * 2 * CELLS : (half + 1) * 2 * CELLS]
            .astype(F32)
            .reshape(2, TILE, TILE, K)
            .astype(BF16)
        )
    pltpu.make_async_copy(x_out.at[everyone], x_out.at[everyone], tile_sems.at[0]).wait()

    def passed_on(step, carry):
        other = lax.rem(row + step, N)

        @pl.when(other != col)
        def _():
            col_copy(site_in, mirror_in, MIRROR, other, col, plain).wait_send()

        return carry

    lax.fori_loop(0, N, passed_on, 0)
    rows_left(site_out, site_in, SITE)
    rows_left(ga_out, ga_in, GREEN_A)
    cols_left(gb_out, gb_in, GREEN_B, to_window)
    rows_left(y_out, y_in, INNER)
    cols_left(s_out, s_in, SIGMA, plain)


def sites_of(block):
    run = 32 * np.arange(16)
    if block == 0:
        return np.concatenate([run, 16 + run])
    return np.concatenate([block + run, (-block - run) % K])


def split(matrix):
    high = matrix.astype(jnp.bfloat16)
    low = (matrix - high.astype(np.float64)).astype(jnp.bfloat16)
    return np.concatenate([high, low], axis=-1)


def inverse_block(angle):
    cos, sin = np.cos(angle), np.sin(angle)
    return np.stack([np.stack([cos, sin], -1), np.stack([-sin, cos], -1)], -2)


def constants():
    order = (np.arange(K) // BLOCK) + N * (np.arange(K) % BLOCK)
    sites = np.concatenate([sites_of(block) for block in range(N)])
    phases = (sites[:, None] * order[None, :] % K).astype(np.float32) * np.float32(
        2.0 * math.pi / K
    )
    table = np.concatenate([np.cos(phases), np.sin(phases)], axis=1).astype(jnp.bfloat16)
    inner = np.zeros((N, N, 2, 2, 2, 2, 2, 2, 16))
    for block in range(N):
        near = sites_of(block).reshape(2, 16)
        angle = 2.0 * math.pi / K * (np.arange(N)[:, None, None] * near[None] % K)
        turn = inverse_block(angle)
        for half in range(2):
            for run in range(2):
                inner[block, :, half, :, run, half, :, run, :] = turn[:, run].transpose(0, 2, 3, 1)
    residues = np.array([[0, 16]] + [[b, 32 - b] for b in range(1, N)])
    angle = 2.0 * math.pi / 32 * (np.arange(32)[:, None, None] * residues[None] % 32)
    turn = inverse_block(angle)
    outer = np.zeros((32, 2, 2, N, 2, 2, 2))
    for half in range(2):
        outer[:, half, :, :, half] = turn.transpose(0, 3, 1, 4, 2)
    return table, split(inner.reshape(N, LANES, LANES)), split(outer.reshape(LANES, LANES))


def body(green_lesser, green_greater, lattice_map, time_offset):
    hbm = pl.BlockSpec(memory_space=pltpu.MemorySpace.HBM)
    vmem = pl.BlockSpec(memory_space=pltpu.MemorySpace.VMEM)
    tile = jax.ShapeDtypeStruct((2, TILE, TILE, K), BF16)
    by_row = pltpu.VMEM((N, 2, BLOCK, LANES), BF16)
    by_col = pltpu.VMEM((N, 2, 4, TILE, LANES), BF16)
    wide = pltpu.VMEM((N, TILE, WIDE), BF16)
    window = pltpu.VMEM((2, 4, N, TILE, LANES), BF16)
    halves = pltpu.VMEM((2, 2 * BLOCK, WIDE), BF16)
    return pl.pallas_call(
        kernel,
        out_shape=(tile, tile),
        in_specs=[pl.BlockSpec(memory_space=pltpu.MemorySpace.SMEM)] + [hbm] * 6,
        out_specs=(vmem, vmem),
        scratch_shapes=[
            pltpu.VMEM((1, K), jnp.int32),
            pltpu.VMEM((2, 2, TILE, TILE, K), BF16),
            pltpu.VMEM((K, 2 * K), BF16),
            pltpu.VMEM((LANES, 2 * LANES), BF16),
            pltpu.VMEM((LANES, 2 * LANES), BF16),
            pltpu.VMEM((K, K), BF16),
            pltpu.VMEM((2 * K, LANES), F32),
            halves, halves,
            pltpu.VMEM((LANES, WIDE), BF16),
            by_row, by_row, by_row,
            wide, wide, wide, wide,
            by_row, by_row, by_col, window,
            pltpu.VMEM((2, 2, 2 * LANES, 4 * LANES), BF16),
            pltpu.VMEM((2 * K, LANES), F32),
            pltpu.VMEM((K, K), BF16),
            pltpu.VMEM((N * N, 4, LANES), BF16),
            pltpu.VMEM((N * N, 4, LANES), BF16),
            pltpu.SemaphoreType.DMA((6,)),
            pltpu.SemaphoreType.DMA((6, N)),
            pltpu.SemaphoreType.DMA((6, N)),
            pltpu.SemaphoreType.DMA((2,)),
        ],
        compiler_params=pltpu.CompilerParams(
            collective_id=0, has_side_effects=True, vmem_limit_bytes=32 * 1024 * 1024
        ),
    )(
        time_offset,
        *(
            pltpu.with_memory_space_constraint(value, pltpu.MemorySpace.HBM)
            for value in (
                lattice_map.reshape(1, K), green_lesser, green_greater,
                *(jnp.asarray(value) for value in constants()),
            )
        ),
    )


def solution(mesh):
    in_specs = (P(None, "trow", "tcol", None), P(None, "trow", "tcol", None), P(), P())
    out_specs = (P(None, "trow", "tcol", None), P(None, "trow", "tcol", None))
    return jax.shard_map(body, mesh=mesh, in_specs=in_specs, out_specs=out_specs, check_vma=False)
```

```python
import math

import jax
import jax.numpy as jnp
import numpy as np
from jax import lax
from jax.experimental import pallas as pl
from jax.experimental.pallas import tpu as pltpu
from jax.sharding import PartitionSpec as P

PERIOD = 64
STEP_SIZE = 0.01
DRIVE_DEPTH = 0.5
MESH = pl.DeviceIdType.MESH
F32 = jnp.float32
BF16 = jnp.bfloat16

N = 16
TILE = 8
K = 512
BLOCK = K // N
LANES = N * TILE
WIDE = TILE * LANES
CELLS = TILE * TILE
NORM = 1.0 / math.sqrt(K)

NT = (((1,), (1,)), ((), ()))
NN = (((1,), (0,)), ((), ()))

SITE, MIRROR, INNER, SIGMA, GREEN_A, GREEN_B = range(6)

ROW_OFFSETS = sorted(
    ((x, y, c) for x in (2, 1, -1, 0) for y in (1, 0) for c in (0, 1)),
    key=lambda o: -(abs(o[0]) + o[1] + 0.2 * o[2]),
)[:-1]
COL_OFFSETS = sorted(
    ((y, z) for z in (4, 3, -3, 2, -2, 1, -1, 0) for y in (1, 0)),
    key=lambda o: -(abs(o[1]) + 2 * o[0]),
)


def row_at(row, offset, sign=1):
    x, y, c = row // 4, (row // 2) % 2, row % 2
    dx, dy, dc = offset
    return ((x + sign * dx + 4) % 4) * 4 + ((y + dy) % 2) * 2 + (c + dc) % 2


def col_at(col, offset, sign=1):
    y, z = col // 8, col % 8
    dy, dz = offset
    return ((y + dy) % 2) * 8 + (z + sign * dz + 8) % 8


def mm(left, right, dims=NN):
    return lax.dot_general(left, right, dims, preferred_element_type=F32)


def block_swap(parts):
    parts = list(parts)
    lane = lax.broadcasted_iota(jnp.int32, parts[0].shape, 1)
    bit = 1
    while bit < N:
        shift = bit * TILE
        low = (lane // shift) % 2 == 0
        for i in range(N):
            if i & bit:
                continue
            first, second = parts[i], parts[i | bit]
            parts[i] = jnp.where(low, first, pltpu.roll(second, shift, 1))
            parts[i | bit] = jnp.where(low, pltpu.roll(first, LANES - shift, 1), second)
        bit *= 2
    return parts


def one_hot(hit):
    return jnp.where(hit, 1.0, 0.0).astype(BF16)


def kernel(
    offset_ref, map_hbm, lesser_hbm, greater_hbm, table_hbm, inner_hbm, outer_hbm,
    out_lesser, out_greater,
    momentum_map, green, table, inner, outer, perm, spread, own, mirror, selves,
    site_out, site_in, mirror_in, y_out, y_in, s_out, s_in,
    ga_out, ga_in, gb_out, gb_in, lefts, results, select, x_out, x_in,
    load_sems, send_sems, recv_sems, tile_sems,
):
    row = lax.axis_index("trow")
    col = lax.axis_index("tcol")
    barrier = pltpu.get_barrier_semaphore()
    row_to = [row_at(row, offset) for offset in ROW_OFFSETS]
    row_from = [row_at(row, offset, -1) for offset in ROW_OFFSETS]
    col_to = [col_at(col, offset) for offset in COL_OFFSETS[:-1]]
    col_from = [col_at(col, offset, -1) for offset in COL_OFFSETS[:-1]]

    loads = [
        pltpu.make_async_copy(source, target, load_sems.at[i])
        for i, (source, target) in enumerate(
            (
                (map_hbm, momentum_map),
                (lesser_hbm, green.at[0]),
                (greater_hbm, green.at[1]),
                (table_hbm, table),
                (outer_hbm, outer),
                (inner_hbm.at[row], inner),
            )
        )
    ]
    for load in loads:
        load.start()
    for other in col_to:
        pl.semaphore_signal(barrier, inc=1, device_id=(row, other), device_id_type=MESH)
    for other in row_to:
        pl.semaphore_signal(barrier, inc=1, device_id=(other, col), device_id_type=MESH)

    def row_copy(source, target, phase, other, slot):
        return pltpu.make_async_remote_copy(
            src_ref=source.at[other], dst_ref=target.at[slot],
            send_sem=send_sems.at[phase, other], recv_sem=recv_sems.at[phase, slot],
            device_id=(other, col), device_id_type=MESH,
        )

    def along_rows(source, target, phase):
        for other in row_to:
            row_copy(source, target, phase, other, row).start()
        target[pl.ds(row, 1)] = source[pl.ds(row, 1)]

    def rows_arrived(source, target, phase):
        for other in row_from:
            row_copy(source, target, phase, other, other).wait_recv()

    def rows_left(source, target, phase):
        for other in row_to:
            row_copy(source, target, phase, other, row).wait_send()

    plain = (lambda ref, i: ref.at[i], lambda ref, i: ref.at[i])
    to_window = (lambda ref, i: ref.at[i], lambda ref, i: ref.at[:, :, i])

    def col_copy(source, target, phase, other, slot, form):
        return pltpu.make_async_remote_copy(
            src_ref=form[0](source, other), dst_ref=form[1](target, slot),
            send_sem=send_sems.at[phase, other], recv_sem=recv_sems.at[phase, slot],
            device_id=(row, other), device_id_type=MESH,
        )

    def along_cols(source, target, phase, form):
        for other in col_to:
            col_copy(source, target, phase, other, col, form).start()

    def cols_arrived(source, target, phase, form):
        for other in col_from:
            col_copy(source, target, phase, other, other, form).wait_recv()

    def cols_left(source, target, phase, form):
        for other in col_to:
            col_copy(source, target, phase, other, col, form).wait_send()

    place = lax.broadcasted_iota(jnp.int32, (K, 1), 0)
    loads[0].wait()
    perm[...] = one_hot((place // BLOCK) + N * (place % BLOCK) == momentum_map[...])
    r = lax.broadcasted_iota(jnp.int32, (LANES, LANES), 0)
    c = lax.broadcasted_iota(jnp.int32, (LANES, LANES), 1)
    swap = one_hot(
        (r // CELLS == c // CELLS)
        & ((r // TILE) % TILE == c % TILE)
        & (r % TILE == (c // TILE) % TILE)
    )

    loads[1].wait()
    loads[2].wait()
    turned = []
    pairs = []
    for half in range(2):
        natural = green[half].astype(F32).reshape(2 * CELLS, K).astype(BF16)
        turned.append(mm(swap, natural).astype(BF16))
    turned = jnp.concatenate(turned, axis=0)
    ordered = mm(turned, perm[...], NT)
    for half in range(2):
        g_re = ordered[2 * half * CELLS : (2 * half + 1) * CELLS]
        g_im = ordered[(2 * half + 1) * CELLS : (2 * half + 2) * CELLS]
        pairs.append(jnp.concatenate([g_re, -g_im], axis=1))
        pairs.append(jnp.concatenate([g_im, g_re], axis=1))
    pairs = jnp.concatenate(pairs, axis=0).astype(BF16)
    loads[3].wait()
    sites = mm(table[...], pairs, NT) * NORM
    for half in range(2):
        site_out[:, half] = (
            sites[:, half * LANES : (half + 1) * LANES].reshape(N, BLOCK, LANES).astype(BF16)
        )

    pl.semaphore_wait(barrier, 2 * (N - 1))
    along_rows(site_out, site_in, SITE)
    spectral = mm(perm[...], turned, NT)
    for half in range(2):
        ga_out[:, half] = (
            spectral[:, half * LANES : (half + 1) * LANES].reshape(N, BLOCK, LANES).astype(BF16)
        )

    def pass_on(other):
        @pl.when(other != col)
        def _():
            col_copy(site_in, mirror_in, MIRROR, other, col, plain).start()

        @pl.when(other == col)
        def _():
            mirror_in[pl.ds(col, 1)] = site_in[pl.ds(col, 1)]

    pass_on(row)

    for other in row_from:
        row_copy(site_out, site_in, SITE, other, other).wait_recv()
        pass_on(other)
    along_rows(ga_out, ga_in, GREEN_A)

    for half in range(2):
        for part in range(2):
            base = part * 16
            swapped = block_swap(
                [site_in[a, half, base : base + 16, :].astype(F32) for a in range(N)]
            )
            for q in range(N):
                at, lane = (q // TILE) * BLOCK + base, (q % TILE) * LANES
                own[half, at : at + 16, lane : lane + LANES] = swapped[q].astype(BF16)

    rows_arrived(ga_out, ga_in, GREEN_A)
    for half in range(2):
        for part in range(2):
            base = part * 16
            swapped = block_swap(
                [ga_in[a, half, base : base + 16, :].astype(F32) for a in range(N)]
            )
            for q in range(N):
                start = (half * N + q) * BLOCK + base
                spread[start : start + 16, :] = swapped[q]
    for m in range(BLOCK):
        picked = spread[pl.ds(m, BLOCK, stride=BLOCK), :]
        gb_out[m // 2, m % 2] = picked.reshape(4, TILE, LANES).astype(BF16)
    gb_in[:, :, pl.ds(col, 1)] = gb_out[pl.ds(col, 1)].reshape(2, 4, 1, TILE, LANES)

    steps = lax.broadcasted_iota(jnp.int32, (TILE, LANES), 1)
    late = lax.broadcasted_iota(jnp.int32, (TILE, LANES), 0) + col * TILE

    def drive(at):
        phase = ((offset_ref[0] + at) % PERIOD).astype(F32) * (2.0 * math.pi / PERIOD)
        return 1.0 + DRIVE_DEPTH * jnp.cos(phase)

    product = drive(late) * drive(steps)
    coupling = jnp.concatenate([product[i : i + 1] for i in range(TILE)], axis=1)
    fr = lax.broadcasted_iota(jnp.int32, (2 * BLOCK, 2 * BLOCK), 0)
    fc = lax.broadcasted_iota(jnp.int32, (2 * BLOCK, 2 * BLOCK), 1)
    first_run = (fc // 16) % 2 == 0
    inside = fc + jnp.where(first_run, 16, -16)
    edge = (fc // 16) * 16 + jnp.where(first_run, (16 - fc % 16) % 16, 15 - fc % 16)
    flip = one_hot(fr == inside + jnp.where(row == 0, 1, 0) * (edge - inside))

    along_cols(gb_out, gb_in, GREEN_B, to_window)
    cols_arrived(site_in, mirror_in, MIRROR, plain)
    spread[...] = mm(mirror_in[...].reshape(2 * K, LANES), swap)
    for half in range(2):
        for part in range(2):
            base = part * 16
            swapped = block_swap(
                [
                    spread[pl.ds(b * 2 * BLOCK + half * BLOCK + base, 16), :]
                    for b in range(N)
                ]
            )
            for q in range(N):
                at, lane = (q // TILE) * BLOCK + base, (q % TILE) * LANES
                mirror[half, at : at + 16, lane : lane + LANES] = swapped[q].astype(BF16)
    for half in range(2):
        first_re, first_im = own[half, :BLOCK].astype(F32), own[half, BLOCK:].astype(F32)
        other = mm(flip, mirror[1 - half])
        other_re, other_im = other[:BLOCK], other[BLOCK:]
        square_re = first_re * first_re - first_im * first_im
        square_im = 2.0 * first_re * first_im
        self_re = coupling * (square_re * other_re - square_im * other_im)
        self_im = coupling * (square_re * other_im + square_im * other_re)
        at = half * 2 * BLOCK
        selves[at : at + BLOCK] = self_re.astype(BF16)
        selves[at + BLOCK : at + 2 * BLOCK] = self_im.astype(BF16)
    doubled = jnp.concatenate([selves[...], selves[...]], axis=0)
    loads[5].wait()
    y_out[...] = mm(inner[...], doubled).reshape(N, TILE, WIDE).astype(BF16)
    along_rows(y_out, y_in, INNER)

    down = lax.broadcasted_iota(jnp.int32, (LANES, LANES), 0)
    across = lax.broadcasted_iota(jnp.int32, (LANES, LANES), 1)
    cols_arrived(gb_out, gb_in, GREEN_B, to_window)
    for k in range(2):
        g = [gb_in[k, i].astype(F32).reshape(LANES, LANES) for i in range(4)]
        advanced = [jnp.where(across <= down, g[i] - g[2 + i], 0.0) for i in range(2)]
        for half in range(2):
            g_re, g_im = g[2 * half], g[2 * half + 1]
            for i, blocks in enumerate(
                ([g_re, -g_im, advanced[0], -advanced[1]], [g_im, g_re, advanced[1], advanced[0]])
            ):
                lefts[k, half, i * LANES : (i + 1) * LANES, :] = jnp.concatenate(
                    blocks, axis=1
                ).astype(BF16)

    loads[4].wait()
    rows_arrived(y_out, y_in, INNER)
    arrived = y_in[...].astype(F32).reshape(LANES, WIDE).astype(BF16)
    sigma = mm(outer[...], jnp.concatenate([arrived, arrived], axis=0)) * NORM
    s_out[...] = sigma.reshape(N, TILE, WIDE).astype(BF16)
    along_cols(s_out, s_in, SIGMA, plain)
    s_in[pl.ds(col, 1)] = s_out[pl.ds(col, 1)]
    cols_arrived(s_out, s_in, SIGMA, plain)
    for b in range(N):
        for t in range(TILE):
            start = (b * TILE + t) * TILE
            spread[start : start + TILE, :] = s_in[b, :, t * LANES : (t + 1) * LANES].astype(F32)
    for k in range(2):
        s = [spread[pl.ds(4 * k + i, LANES, stride=TILE), :] for i in range(4)]
        retarded = [jnp.where(down <= across, s[2 + i] - s[i], 0.0) for i in range(2)]
        for half in range(2):
            right = jnp.concatenate(
                retarded + [s[2 * half], s[2 * half + 1]], axis=0
            ).astype(BF16)
            total = mm(lefts[k, half], right) * STEP_SIZE
            start = (4 * k + 2 * half) * LANES
            results[start : start + 2 * LANES, :] = total

    for piece in range(4):
        swapped = block_swap(
            [
                results[pl.ds((q // 2) * LANES + q % 2 + 32 * piece, 16, stride=2), :]
                for q in range(N)
            ]
        )
        for a in range(N):
            start = a * N + 4 * piece
            x_out[start : start + 4] = swapped[a].reshape(4, 4, LANES).astype(BF16)
    me = row * N + col

    def tile_copy(other_row, other_col):
        return pltpu.make_async_remote_copy(
            src_ref=x_out.at[other_row * N + other_col], dst_ref=x_in.at[me],
            send_sem=tile_sems.at[0], recv_sem=tile_sems.at[1],
            device_id=(other_row, other_col), device_id_type=MESH,
        )

    row_ids = row_to + [row]
    col_ids = col_to + [col]
    row_far = [abs(o[0]) + o[1] + 0.2 * o[2] for o in ROW_OFFSETS] + [0.0]
    col_far = [abs(o[1]) + 2 * o[0] for o in COL_OFFSETS]
    order = sorted(
        ((i, j) for j in range(N) for i in range(N)), key=lambda p: -(row_far[p[0]] + col_far[p[1]])
    )[:-1]
    for i, j in order:
        tile_copy(row_ids[i], col_ids[j]).start()
    x_in[pl.ds(me, 1)] = x_out[pl.ds(me, 1)]

    place = lax.broadcasted_iota(jnp.int32, (K, 1), 0)
    member, device = place // (N * N), place % (N * N)
    perm[...] = one_hot(
        device // N + N * (2 * (device % N) + member) == momentum_map[...]
    )
    part, early, late = (place // CELLS) % 4, (place // TILE) % TILE, place % TILE
    lane = (late // 2) * LANES + ((member * 4 + part) * 2 + late % 2) * TILE + early
    select[...] = one_hot(lane == lax.broadcasted_iota(jnp.int32, (1, K), 1))
    def passed_on(step, carry):
        other = lax.rem(row + step, N)

        @pl.when(other != col)
        def _():
            col_copy(site_in, mirror_in, MIRROR, other, col, plain).wait_send()

        return carry

    lax.fori_loop(0, N, passed_on, 0)
    rows_left(site_out, site_in, SITE)
    rows_left(ga_out, ga_in, GREEN_A)
    cols_left(gb_out, gb_in, GREEN_B, to_window)
    rows_left(y_out, y_in, INNER)
    cols_left(s_out, s_in, SIGMA, plain)

    everyone = pl.ds(0, N * N - 1)
    pltpu.make_async_copy(x_in.at[everyone], x_in.at[everyone], tile_sems.at[1]).wait()
    for d in range(N * N):
        spread[4 * d : 4 * d + 4, :] = x_in[d].astype(F32)
    rows = jnp.concatenate(
        [spread[pl.ds(i, N * N, stride=4), :] for i in range(4)], axis=1
    ).astype(BF16)
    cells = mm(select[...], rows, NT).astype(BF16)
    cells = jnp.concatenate([cells[: K // 2], cells[K // 2 :]], axis=1)
    final = mm(cells, perm[...]).astype(BF16)
    for half, out in enumerate((out_lesser, out_greater)):
        out[...] = (
            final[half * 2 * CELLS : (half + 1) * 2 * CELLS]
            .astype(F32)
            .reshape(2, TILE, TILE, K)
            .astype(BF16)
        )
    pltpu.make_async_copy(x_out.at[everyone], x_out.at[everyone], tile_sems.at[0]).wait()


def sites_of(block):
    run = 32 * np.arange(16)
    if block == 0:
        return np.concatenate([run, 16 + run])
    return np.concatenate([block + run, (-block - run) % K])


def split(matrix):
    high = matrix.astype(jnp.bfloat16)
    low = (matrix - high.astype(np.float64)).astype(jnp.bfloat16)
    return np.concatenate([high, low], axis=-1)


def inverse_block(angle):
    cos, sin = np.cos(angle), np.sin(angle)
    return np.stack([np.stack([cos, sin], -1), np.stack([-sin, cos], -1)], -2)


def constants():
    order = (np.arange(K) // BLOCK) + N * (np.arange(K) % BLOCK)
    sites = np.concatenate([sites_of(block) for block in range(N)])
    phases = (sites[:, None] * order[None, :] % K).astype(np.float32) * np.float32(
        2.0 * math.pi / K
    )
    table = np.concatenate([np.cos(phases), np.sin(phases)], axis=1).astype(jnp.bfloat16)
    inner = np.zeros((N, N, 2, 2, 2, 2, 2, 2, 16))
    for block in range(N):
        near = sites_of(block).reshape(2, 16)
        angle = 2.0 * math.pi / K * (np.arange(N)[:, None, None] * near[None] % K)
        turn = inverse_block(angle)
        for half in range(2):
            for run in range(2):
                inner[block, :, half, :, run, half, :, run, :] = turn[:, run].transpose(0, 2, 3, 1)
    residues = np.array([[0, 16]] + [[b, 32 - b] for b in range(1, N)])
    angle = 2.0 * math.pi / 32 * (np.arange(32)[:, None, None] * residues[None] % 32)
    turn = inverse_block(angle)
    outer = np.zeros((32, 2, 2, N, 2, 2, 2))
    for half in range(2):
        outer[:, half, :, :, half] = turn.transpose(0, 3, 1, 4, 2)
    return table, split(inner.reshape(N, LANES, LANES)), split(outer.reshape(LANES, LANES))


def body(green_lesser, green_greater, lattice_map, time_offset):
    hbm = pl.BlockSpec(memory_space=pltpu.MemorySpace.HBM)
    vmem = pl.BlockSpec(memory_space=pltpu.MemorySpace.VMEM)
    tile = jax.ShapeDtypeStruct((2, TILE, TILE, K), BF16)
    by_row = pltpu.VMEM((N, 2, BLOCK, LANES), BF16)
    by_col = pltpu.VMEM((N, 2, 4, TILE, LANES), BF16)
    wide = pltpu.VMEM((N, TILE, WIDE), BF16)
    window = pltpu.VMEM((2, 4, N, TILE, LANES), BF16)
    halves = pltpu.VMEM((2, 2 * BLOCK, WIDE), BF16)
    return pl.pallas_call(
        kernel,
        out_shape=(tile, tile),
        in_specs=[pl.BlockSpec(memory_space=pltpu.MemorySpace.SMEM)] + [hbm] * 6,
        out_specs=(vmem, vmem),
        scratch_shapes=[
            pltpu.VMEM((1, K), jnp.int32),
            pltpu.VMEM((2, 2, TILE, TILE, K), BF16),
            pltpu.VMEM((K, 2 * K), BF16),
            pltpu.VMEM((LANES, 2 * LANES), BF16),
            pltpu.VMEM((LANES, 2 * LANES), BF16),
            pltpu.VMEM((K, K), BF16),
            pltpu.VMEM((2 * K, LANES), F32),
            halves, halves,
            pltpu.VMEM((LANES, WIDE), BF16),
            by_row, by_row, by_row,
            wide, wide, wide, wide,
            by_row, by_row, by_col, window,
            pltpu.VMEM((2, 2, 2 * LANES, 4 * LANES), BF16),
            pltpu.VMEM((2 * K, LANES), F32),
            pltpu.VMEM((K, K), BF16),
            pltpu.VMEM((N * N, 4, LANES), BF16),
            pltpu.VMEM((N * N, 4, LANES), BF16),
            pltpu.SemaphoreType.DMA((6,)),
            pltpu.SemaphoreType.DMA((6, N)),
            pltpu.SemaphoreType.DMA((6, N)),
            pltpu.SemaphoreType.DMA((2,)),
        ],
        compiler_params=pltpu.CompilerParams(
            collective_id=0, has_side_effects=True, vmem_limit_bytes=32 * 1024 * 1024
        ),
    )(
        time_offset,
        *(
            pltpu.with_memory_space_constraint(value, pltpu.MemorySpace.HBM)
            for value in (
                lattice_map.reshape(1, K), green_lesser, green_greater,
                *(jnp.asarray(value) for value in constants()),
            )
        ),
    )


def solution(mesh):
    in_specs = (P(None, "trow", "tcol", None), P(None, "trow", "tcol", None), P(), P())
    out_specs = (P(None, "trow", "tcol", None), P(None, "trow", "tcol", None))
    return jax.shard_map(body, mesh=mesh, in_specs=in_specs, out_specs=out_specs, check_vma=False)
```

```python
import math

import jax
import jax.numpy as jnp
import numpy as np
from jax import lax
from jax.experimental import pallas as pl
from jax.experimental.pallas import tpu as pltpu
from jax.sharding import PartitionSpec as P

PERIOD = 64
STEP_SIZE = 0.01
DRIVE_DEPTH = 0.5
MESH = pl.DeviceIdType.MESH
F32 = jnp.float32
BF16 = jnp.bfloat16

N = 16
TILE = 8
K = 512
BLOCK = K // N
LANES = N * TILE
WIDE = TILE * LANES
CELLS = TILE * TILE
NORM = 1.0 / math.sqrt(K)

NT = (((1,), (1,)), ((), ()))
NN = (((1,), (0,)), ((), ()))

SITE, MIRROR, INNER, SIGMA, GREEN_A, GREEN_B = range(6)

ROW_OFFSETS = sorted(
    ((x, y, c) for x in (2, 1, -1, 0) for y in (1, 0) for c in (0, 1)),
    key=lambda o: -(abs(o[0]) + o[1] + 0.2 * o[2]),
)[:-1]
COL_OFFSETS = sorted(
    ((y, z) for z in (4, 3, -3, 2, -2, 1, -1, 0) for y in (1, 0)),
    key=lambda o: -(abs(o[1]) + 2 * o[0]),
)


def row_at(row, offset, sign=1):
    x, y, c = row // 4, (row // 2) % 2, row % 2
    dx, dy, dc = offset
    return ((x + sign * dx + 4) % 4) * 4 + ((y + dy) % 2) * 2 + (c + dc) % 2


def col_at(col, offset, sign=1):
    y, z = col // 8, col % 8
    dy, dz = offset
    return ((y + dy) % 2) * 8 + (z + sign * dz + 8) % 8


def mm(left, right, dims=NN):
    return lax.dot_general(left, right, dims, preferred_element_type=F32)


def block_swap(parts):
    parts = list(parts)
    lane = lax.broadcasted_iota(jnp.int32, parts[0].shape, 1)
    bit = 1
    while bit < N:
        shift = bit * TILE
        low = (lane // shift) % 2 == 0
        for i in range(N):
            if i & bit:
                continue
            first, second = parts[i], parts[i | bit]
            parts[i] = jnp.where(low, first, pltpu.roll(second, shift, 1))
            parts[i | bit] = jnp.where(low, pltpu.roll(first, LANES - shift, 1), second)
        bit *= 2
    return parts


def one_hot(hit):
    return jnp.where(hit, 1.0, 0.0).astype(BF16)


def kernel(
    offset_ref, map_hbm, lesser_hbm, greater_hbm, table_hbm, inner_hbm, outer_hbm,
    out_lesser, out_greater,
    momentum_map, green, table, inner, outer, perm, spread, own, mirror, selves,
    site_out, site_in, mirror_in, y_out, y_in, s_out, s_in,
    ga_out, ga_in, gb_out, gb_in, lefts, results, select, x_out, x_in,
    load_sems, send_sems, recv_sems, tile_sems,
):
    row = lax.axis_index("trow")
    col = lax.axis_index("tcol")
    barrier = pltpu.get_barrier_semaphore()
    row_to = [row_at(row, offset) for offset in ROW_OFFSETS]
    row_from = [row_at(row, offset, -1) for offset in ROW_OFFSETS]
    col_to = [col_at(col, offset) for offset in COL_OFFSETS[:-1]]
    col_from = [col_at(col, offset, -1) for offset in COL_OFFSETS[:-1]]

    loads = [
        pltpu.make_async_copy(source, target, load_sems.at[i])
        for i, (source, target) in enumerate(
            (
                (map_hbm, momentum_map),
                (lesser_hbm, green.at[0]),
                (greater_hbm, green.at[1]),
                (table_hbm, table),
                (outer_hbm, outer),
                (inner_hbm.at[row], inner),
            )
        )
    ]
    for load in loads:
        load.start()
    for other in col_to:
        pl.semaphore_signal(barrier, inc=1, device_id=(row, other), device_id_type=MESH)
    for other in row_to:
        pl.semaphore_signal(barrier, inc=1, device_id=(other, col), device_id_type=MESH)

    def row_copy(source, target, phase, other, slot):
        return pltpu.make_async_remote_copy(
            src_ref=source.at[other], dst_ref=target.at[slot],
            send_sem=send_sems.at[phase, other], recv_sem=recv_sems.at[phase, slot],
            device_id=(other, col), device_id_type=MESH,
        )

    def along_rows(source, target, phase):
        for other in row_to:
            row_copy(source, target, phase, other, row).start()
        target[pl.ds(row, 1)] = source[pl.ds(row, 1)]

    def rows_arrived(source, target, phase):
        for other in row_from:
            row_copy(source, target, phase, other, other).wait_recv()

    def rows_left(source, target, phase):
        for other in row_to:
            row_copy(source, target, phase, other, row).wait_send()

    plain = (lambda ref, i: ref.at[i], lambda ref, i: ref.at[i])

    def col_copy(source, target, phase, other, slot, form):
        return pltpu.make_async_remote_copy(
            src_ref=form[0](source, other), dst_ref=form[1](target, slot),
            send_sem=send_sems.at[phase, other], recv_sem=recv_sems.at[phase, slot],
            device_id=(row, other), device_id_type=MESH,
        )

    def along_cols(source, target, phase, form):
        for other in col_to:
            col_copy(source, target, phase, other, col, form).start()

    def cols_arrived(source, target, phase, form):
        for other in col_from:
            col_copy(source, target, phase, other, other, form).wait_recv()

    def cols_left(source, target, phase, form):
        for other in col_to:
            col_copy(source, target, phase, other, col, form).wait_send()

    place = lax.broadcasted_iota(jnp.int32, (K, 1), 0)
    loads[0].wait()
    perm[...] = one_hot((place // BLOCK) + N * (place % BLOCK) == momentum_map[...])
    r = lax.broadcasted_iota(jnp.int32, (LANES, LANES), 0)
    c = lax.broadcasted_iota(jnp.int32, (LANES, LANES), 1)
    swap = one_hot(
        (r // CELLS == c // CELLS)
        & ((r // TILE) % TILE == c % TILE)
        & (r % TILE == (c // TILE) % TILE)
    )

    loads[1].wait()
    loads[2].wait()
    turned = []
    pairs = []
    for half in range(2):
        natural = green[half].astype(F32).reshape(2 * CELLS, K).astype(BF16)
        turned.append(mm(swap, natural).astype(BF16))
    turned = jnp.concatenate(turned, axis=0)
    ordered = mm(turned, perm[...], NT)
    for half in range(2):
        g_re = ordered[2 * half * CELLS : (2 * half + 1) * CELLS]
        g_im = ordered[(2 * half + 1) * CELLS : (2 * half + 2) * CELLS]
        pairs.append(jnp.concatenate([g_re, -g_im], axis=1))
        pairs.append(jnp.concatenate([g_im, g_re], axis=1))
    pairs = jnp.concatenate(pairs, axis=0).astype(BF16)
    loads[3].wait()
    sites = mm(table[...], pairs, NT) * NORM
    for half in range(2):
        site_out[:, half] = (
            sites[:, half * LANES : (half + 1) * LANES].reshape(N, BLOCK, LANES).astype(BF16)
        )

    pl.semaphore_wait(barrier, 2 * (N - 1))
    along_rows(site_out, site_in, SITE)
    spectral = mm(perm[...], turned, NT)
    for half in range(2):
        ga_out[:, half] = (
            spectral[:, half * LANES : (half + 1) * LANES].reshape(N, BLOCK, LANES).astype(BF16)
        )

    def pass_on(other):
        @pl.when(other != col)
        def _():
            col_copy(site_in, mirror_in, MIRROR, other, col, plain).start()

        @pl.when(other == col)
        def _():
            mirror_in[pl.ds(col, 1)] = site_in[pl.ds(col, 1)]

    pass_on(row)

    for other in row_from:
        row_copy(site_out, site_in, SITE, other, other).wait_recv()
        pass_on(other)
    along_rows(ga_out, ga_in, GREEN_A)

    for half in range(2):
        for part in range(2):
            base = part * 16
            swapped = block_swap(
                [site_in[a, half, base : base + 16, :].astype(F32) for a in range(N)]
            )
            for q in range(N):
                at, lane = (q // TILE) * BLOCK + base, (q % TILE) * LANES
                own[half, at : at + 16, lane : lane + LANES] = swapped[q].astype(BF16)

    rows_arrived(ga_out, ga_in, GREEN_A)
    for half in range(2):
        for part in range(2):
            base = part * 16
            swapped = block_swap(
                [ga_in[a, half, base : base + 16, :].astype(F32) for a in range(N)]
            )
            for q in range(N):
                start = (half * N + q) * BLOCK + base
                spread[start : start + 16, :] = swapped[q]
    for m in range(BLOCK):
        picked = spread[pl.ds(m, BLOCK, stride=BLOCK), :]
        gb_out[m // 2, m % 2] = picked.reshape(4, TILE, LANES).astype(BF16)
    gb_in[pl.ds(col, 1)] = gb_out[pl.ds(col, 1)]

    steps = lax.broadcasted_iota(jnp.int32, (TILE, LANES), 1)
    late = lax.broadcasted_iota(jnp.int32, (TILE, LANES), 0) + col * TILE

    def drive(at):
        phase = ((offset_ref[0] + at) % PERIOD).astype(F32) * (2.0 * math.pi / PERIOD)
        return 1.0 + DRIVE_DEPTH * jnp.cos(phase)

    product = drive(late) * drive(steps)
    coupling = jnp.concatenate([product[i : i + 1] for i in range(TILE)], axis=1)
    fr = lax.broadcasted_iota(jnp.int32, (2 * BLOCK, 2 * BLOCK), 0)
    fc = lax.broadcasted_iota(jnp.int32, (2 * BLOCK, 2 * BLOCK), 1)
    first_run = (fc // 16) % 2 == 0
    inside = fc + jnp.where(first_run, 16, -16)
    edge = (fc // 16) * 16 + jnp.where(first_run, (16 - fc % 16) % 16, 15 - fc % 16)
    flip = one_hot(fr == inside + jnp.where(row == 0, 1, 0) * (edge - inside))

    along_cols(gb_out, gb_in, GREEN_B, plain)
    cols_arrived(site_in, mirror_in, MIRROR, plain)
    spread[...] = mm(mirror_in[...].reshape(2 * K, LANES), swap)
    for half in range(2):
        for part in range(2):
            base = part * 16
            swapped = block_swap(
                [
                    spread[pl.ds(b * 2 * BLOCK + half * BLOCK + base, 16), :]
                    for b in range(N)
                ]
            )
            for q in range(N):
                at, lane = (q // TILE) * BLOCK + base, (q % TILE) * LANES
                mirror[half, at : at + 16, lane : lane + LANES] = swapped[q].astype(BF16)
    for half in range(2):
        first_re, first_im = own[half, :BLOCK].astype(F32), own[half, BLOCK:].astype(F32)
        other = mm(flip, mirror[1 - half])
        other_re, other_im = other[:BLOCK], other[BLOCK:]
        square_re = first_re * first_re - first_im * first_im
        square_im = 2.0 * first_re * first_im
        self_re = coupling * (square_re * other_re - square_im * other_im)
        self_im = coupling * (square_re * other_im + square_im * other_re)
        at = half * 2 * BLOCK
        selves[at : at + BLOCK] = self_re.astype(BF16)
        selves[at + BLOCK : at + 2 * BLOCK] = self_im.astype(BF16)
    doubled = jnp.concatenate([selves[...], selves[...]], axis=0)
    loads[5].wait()
    y_out[...] = mm(inner[...], doubled).reshape(N, TILE, WIDE).astype(BF16)
    along_rows(y_out, y_in, INNER)

    down = lax.broadcasted_iota(jnp.int32, (LANES, LANES), 0)
    across = lax.broadcasted_iota(jnp.int32, (LANES, LANES), 1)
    cols_arrived(gb_out, gb_in, GREEN_B, plain)
    for k in range(2):
        g = [
            jnp.concatenate([gb_in[b, k, i].astype(F32) for b in range(N)], axis=0)
            for i in range(4)
        ]
        advanced = [jnp.where(across <= down, g[i] - g[2 + i], 0.0) for i in range(2)]
        for half in range(2):
            g_re, g_im = g[2 * half], g[2 * half + 1]
            for i, blocks in enumerate(
                ([g_re, -g_im, advanced[0], -advanced[1]], [g_im, g_re, advanced[1], advanced[0]])
            ):
                lefts[k, half, i * LANES : (i + 1) * LANES, :] = jnp.concatenate(
                    blocks, axis=1
                ).astype(BF16)

    loads[4].wait()
    rows_arrived(y_out, y_in, INNER)
    arrived = y_in[...].astype(F32).reshape(LANES, WIDE).astype(BF16)
    sigma = mm(outer[...], jnp.concatenate([arrived, arrived], axis=0)) * NORM
    s_out[...] = sigma.reshape(N, TILE, WIDE).astype(BF16)
    along_cols(s_out, s_in, SIGMA, plain)
    s_in[pl.ds(col, 1)] = s_out[pl.ds(col, 1)]
    place = lax.broadcasted_iota(jnp.int32, (K, 1), 0)
    member, device = place // (N * N), place % (N * N)
    perm[...] = one_hot(
        device // N + N * (2 * (device % N) + member) == momentum_map[...]
    )
    part, early, late = (place // CELLS) % 4, (place // TILE) % TILE, place % TILE
    lane = (late // 2) * LANES + ((member * 4 + part) * 2 + late % 2) * TILE + early
    select[...] = one_hot(lane == lax.broadcasted_iota(jnp.int32, (1, K), 1))
    cols_arrived(s_out, s_in, SIGMA, plain)
    for b in range(N):
        for t in range(TILE):
            start = (b * TILE + t) * TILE
            spread[start : start + TILE, :] = s_in[b, :, t * LANES : (t + 1) * LANES].astype(F32)
    for k in range(2):
        s = [spread[pl.ds(4 * k + i, LANES, stride=TILE), :] for i in range(4)]
        retarded = [jnp.where(down <= across, s[2 + i] - s[i], 0.0) for i in range(2)]
        for half in range(2):
            right = jnp.concatenate(
                retarded + [s[2 * half], s[2 * half + 1]], axis=0
            ).astype(BF16)
            total = mm(lefts[k, half], right) * STEP_SIZE
            start = (4 * k + 2 * half) * LANES
            results[start : start + 2 * LANES, :] = total

    for piece in range(4):
        swapped = block_swap(
            [
                results[pl.ds((q // 2) * LANES + q % 2 + 32 * piece, 16, stride=2), :]
                for q in range(N)
            ]
        )
        for a in range(N):
            start = a * N + 4 * piece
            x_out[start : start + 4] = swapped[a].reshape(4, 4, LANES).astype(BF16)
    me = row * N + col

    def tile_copy(other_row, other_col):
        return pltpu.make_async_remote_copy(
            src_ref=x_out.at[other_row * N + other_col], dst_ref=x_in.at[me],
            send_sem=tile_sems.at[0], recv_sem=tile_sems.at[1],
            device_id=(other_row, other_col), device_id_type=MESH,
        )

    row_ids = row_to + [row]
    col_ids = col_to + [col]
    row_far = [abs(o[0]) + o[1] + 0.2 * o[2] for o in ROW_OFFSETS] + [0.0]
    col_far = [abs(o[1]) + 2 * o[0] for o in COL_OFFSETS]
    order = sorted(
        ((i, j) for j in range(N) for i in range(N)), key=lambda p: -(row_far[p[0]] + col_far[p[1]])
    )[:-1]
    for i, j in order:
        tile_copy(row_ids[i], col_ids[j]).start()
    x_in[pl.ds(me, 1)] = x_out[pl.ds(me, 1)]

    def passed_on(step, carry):
        other = lax.rem(row + step, N)

        @pl.when(other != col)
        def _():
            col_copy(site_in, mirror_in, MIRROR, other, col, plain).wait_send()

        return carry

    lax.fori_loop(0, N, passed_on, 0)
    rows_left(site_out, site_in, SITE)
    rows_left(ga_out, ga_in, GREEN_A)
    cols_left(gb_out, gb_in, GREEN_B, plain)
    rows_left(y_out, y_in, INNER)
    cols_left(s_out, s_in, SIGMA, plain)

    everyone = pl.ds(0, N * N - 1)
    pltpu.make_async_copy(x_in.at[everyone], x_in.at[everyone], tile_sems.at[1]).wait()
    for d in range(N * N):
        spread[4 * d : 4 * d + 4, :] = x_in[d].astype(F32)
    rows = jnp.concatenate(
        [spread[pl.ds(i, N * N, stride=4), :] for i in range(4)], axis=1
    ).astype(BF16)
    cells = mm(select[...], rows, NT).astype(BF16)
    cells = jnp.concatenate([cells[: K // 2], cells[K // 2 :]], axis=1)
    final = mm(cells, perm[...]).astype(BF16)
    for half, out in enumerate((out_lesser, out_greater)):
        out[...] = (
            final[half * 2 * CELLS : (half + 1) * 2 * CELLS]
            .astype(F32)
            .reshape(2, TILE, TILE, K)
            .astype(BF16)
        )
    pltpu.make_async_copy(x_out.at[everyone], x_out.at[everyone], tile_sems.at[0]).wait()


def sites_of(block):
    run = 32 * np.arange(16)
    if block == 0:
        return np.concatenate([run, 16 + run])
    return np.concatenate([block + run, (-block - run) % K])


def split(matrix):
    high = matrix.astype(jnp.bfloat16)
    low = (matrix - high.astype(np.float64)).astype(jnp.bfloat16)
    return np.concatenate([high, low], axis=-1)


def inverse_block(angle):
    cos, sin = np.cos(angle), np.sin(angle)
    return np.stack([np.stack([cos, sin], -1), np.stack([-sin, cos], -1)], -2)


def constants():
    order = (np.arange(K) // BLOCK) + N * (np.arange(K) % BLOCK)
    sites = np.concatenate([sites_of(block) for block in range(N)])
    phases = (sites[:, None] * order[None, :] % K).astype(np.float32) * np.float32(
        2.0 * math.pi / K
    )
    table = np.concatenate([np.cos(phases), np.sin(phases)], axis=1).astype(jnp.bfloat16)
    inner = np.zeros((N, N, 2, 2, 2, 2, 2, 2, 16))
    for block in range(N):
        near = sites_of(block).reshape(2, 16)
        angle = 2.0 * math.pi / K * (np.arange(N)[:, None, None] * near[None] % K)
        turn = inverse_block(angle)
        for half in range(2):
            for run in range(2):
                inner[block, :, half, :, run, half, :, run, :] = turn[:, run].transpose(0, 2, 3, 1)
    residues = np.array([[0, 16]] + [[b, 32 - b] for b in range(1, N)])
    angle = 2.0 * math.pi / 32 * (np.arange(32)[:, None, None] * residues[None] % 32)
    turn = inverse_block(angle)
    outer = np.zeros((32, 2, 2, N, 2, 2, 2))
    for half in range(2):
        outer[:, half, :, :, half] = turn.transpose(0, 3, 1, 4, 2)
    return table, split(inner.reshape(N, LANES, LANES)), split(outer.reshape(LANES, LANES))


def body(green_lesser, green_greater, lattice_map, time_offset):
    hbm = pl.BlockSpec(memory_space=pltpu.MemorySpace.HBM)
    vmem = pl.BlockSpec(memory_space=pltpu.MemorySpace.VMEM)
    tile = jax.ShapeDtypeStruct((2, TILE, TILE, K), BF16)
    by_row = pltpu.VMEM((N, 2, BLOCK, LANES), BF16)
    by_col = pltpu.VMEM((N, 2, 4, TILE, LANES), BF16)
    wide = pltpu.VMEM((N, TILE, WIDE), BF16)
    halves = pltpu.VMEM((2, 2 * BLOCK, WIDE), BF16)
    return pl.pallas_call(
        kernel,
        out_shape=(tile, tile),
        in_specs=[pl.BlockSpec(memory_space=pltpu.MemorySpace.SMEM)] + [hbm] * 6,
        out_specs=(vmem, vmem),
        scratch_shapes=[
            pltpu.VMEM((1, K), jnp.int32),
            pltpu.VMEM((2, 2, TILE, TILE, K), BF16),
            pltpu.VMEM((K, 2 * K), BF16),
            pltpu.VMEM((LANES, 2 * LANES), BF16),
            pltpu.VMEM((LANES, 2 * LANES), BF16),
            pltpu.VMEM((K, K), BF16),
            pltpu.VMEM((2 * K, LANES), F32),
            halves, halves,
            pltpu.VMEM((LANES, WIDE), BF16),
            by_row, by_row, by_row,
            wide, wide, wide, wide,
            by_row, by_row, by_col, by_col,
            pltpu.VMEM((2, 2, 2 * LANES, 4 * LANES), BF16),
            pltpu.VMEM((2 * K, LANES), F32),
            pltpu.VMEM((K, K), BF16),
            pltpu.VMEM((N * N, 4, LANES), BF16),
            pltpu.VMEM((N * N, 4, LANES), BF16),
            pltpu.SemaphoreType.DMA((6,)),
            pltpu.SemaphoreType.DMA((6, N)),
            pltpu.SemaphoreType.DMA((6, N)),
            pltpu.SemaphoreType.DMA((2,)),
        ],
        compiler_params=pltpu.CompilerParams(
            collective_id=0, has_side_effects=True, vmem_limit_bytes=32 * 1024 * 1024
        ),
    )(
        time_offset,
        *(
            pltpu.with_memory_space_constraint(value, pltpu.MemorySpace.HBM)
            for value in (
                lattice_map.reshape(1, K), green_lesser, green_greater,
                *(jnp.asarray(value) for value in constants()),
            )
        ),
    )


def solution(mesh):
    in_specs = (P(None, "trow", "tcol", None), P(None, "trow", "tcol", None), P(), P())
    out_specs = (P(None, "trow", "tcol", None), P(None, "trow", "tcol", None))
    return jax.shard_map(body, mesh=mesh, in_specs=in_specs, out_specs=out_specs, check_vma=False)
```
